512 devices in a mesh: tm: 16 (over x, z_hi), tmpl: 32 (over y, z_lo, core).
Axes of the slice: x: 4, y: 4, z: 16 (z_hi: 4, z_lo: 4; z = z_hi * 4 + z_lo), core: 2. Of those that a mesh axis runs over, the one named last changes fastest.
Arguments:
- seismic: bfloat16 [512, 3, 16384], P(('tmpl', 'tm')), may hold values from -6 to 6
- templates: bfloat16 [512, 32, 3, 256], P(('tmpl', 'tm')), may hold values from -0.009765625 to 0.009765625
- moveout: int32 [512, 32], P('tmpl'), may hold values from 0 to 128
- active: int32 [512], P('tmpl'), may hold values 0 or 1
Outputs:
- stack: float32 [32, 16384], P('tmpl', 'tm')
The draws below stay inside these ranges and needn't reach their ends.
All inputs are finite; a program needn't handle non-finite values. No bound on the sum of `active` on one device may be relied on, other than what follows from the above.
Results may differ from the reference program's by a relative error of at most 0.0052.
Values may be sent and summed in bfloat16 or wider, within the bound.
A program may use at most 64 MiB of HBM per device.

```python
import math
import jax
import jax.numpy as jnp
from jax import lax

CH = 3
L = 256
NF = 512
BLK = 128
MS = 128
TPL = 32
STATIONS = 512
TIME = 16384


def set_ends(entries, stream_key, least, top_value):
    place = [jax.random.randint(jax.random.fold_in(stream_key, axis), (), 0, length) for axis, length in enumerate(entries.shape)]
    main_axis = entries.shape.index(max(entries.shape))
    neighbour = place[:main_axis] + [(place[main_axis] + 1) % entries.shape[main_axis]] + place[main_axis + 1:]
    return entries.at[tuple(place)].set(least).at[tuple(neighbour)].set(top_value)


def level_of(own_key, dims, shards, least, largest):
    def one(axis_at, blocks):
        steps = jax.random.uniform(jax.random.fold_in(jax.random.fold_in(own_key, 6), axis_at), (blocks,), jnp.float32, least / len(shards), largest / len(shards))
        return jnp.repeat(jnp.exp(steps), dims[axis_at] // blocks).reshape((-1,) + (1,) * (len(dims) - axis_at - 1))

    level = one(*shards[0])
    for cut in shards[1:]:
        level = level * one(*cut)
    return level


def bell_draw(key, extent, spread, most, cuts=(), kind=jnp.bfloat16):
    level = level_of(key, extent, cuts, -0.22, 0.18) if cuts else 1.0
    values = jax.random.normal(key, extent, jnp.float32) * spread * level
    return jnp.minimum(jnp.maximum(values, -most), most).astype(kind)


def setup_inputs(seed: int = 0) -> dict:
    keys = jax.random.split(jax.random.key(seed), 5)
    return {
        "seismic": bell_draw(keys[0], (STATIONS, CH, TIME), 1.0, 6.0, ((0, 512),)),
        "templates": bell_draw(keys[1], (STATIONS, TPL, CH, L), (L * CH * STATIONS) ** -0.5, 0.009765625, ((0, 512),)),
        "moveout": set_ends(jax.random.randint(keys[2], (STATIONS, TPL), 0, MS + 1), jax.random.fold_in(keys[2], 1), 0, MS).astype(jnp.int32),
        "active": set_ends((jax.random.randint(keys[3], (STATIONS,), 0, 4) < 3).astype(jnp.int32), jax.random.fold_in(keys[3], 1), 0, 1),
    }


def forward_table(count, size):
    sample = jnp.arange(count, dtype=jnp.int32)[:, None]
    freq = jnp.arange(size, dtype=jnp.int32)[None, :]
    angle = (2.0 * math.pi / size) * ((sample * freq) % size).astype(jnp.float32)
    return jnp.concatenate([jnp.cos(angle), -jnp.sin(angle)], axis=1).astype(jnp.bfloat16)


def inverse_table(size, outputs):
    freq = jnp.arange(size, dtype=jnp.int32)[:, None]
    lag = jnp.arange(outputs, dtype=jnp.int32)[None, :]
    angle = (2.0 * math.pi / size) * ((freq * lag) % size).astype(jnp.float32)
    return jnp.concatenate([jnp.cos(angle), -jnp.sin(angle)], axis=0) / size


def framed(signal, blocks):
    leading = signal.shape[:-1]
    pieces = signal.reshape(leading + (signal.shape[-1] // BLK, BLK))
    return jnp.concatenate([pieces[..., offset:offset + blocks, :] for offset in range(NF // BLK)], axis=-1)


def station_spectrum(wave, shift_row, active_flag, table, size):
    count_tmpl, chans, length = wave.shape
    spectrum = jnp.dot(wave.reshape(count_tmpl * chans, length), table, preferred_element_type=jnp.float32)
    spectrum = spectrum.reshape(count_tmpl, chans, 2 * size)
    real_part = spectrum[..., :size]
    imag_part = spectrum[..., size:]
    freq = jnp.arange(size, dtype=jnp.int32)[None, :]
    angle = (2.0 * math.pi / size) * ((shift_row[:, None] * freq) % size).astype(jnp.float32)
    cosine = jnp.cos(angle)[:, None, :]
    sine = jnp.sin(angle)[:, None, :]
    weight = active_flag.astype(jnp.float32)
    out_real = (real_part * cosine + imag_part * sine) * weight
    out_imag = (real_part * sine - imag_part * cosine) * weight
    return jnp.concatenate([out_real, out_imag], axis=-1).astype(jnp.bfloat16)


def reference(seismic, templates, moveout, active):
    blocks = TIME // BLK
    data_table = forward_table(NF, NF)
    tmpl_table = forward_table(L, NF)
    padded = jnp.concatenate([seismic, jnp.zeros((STATIONS, CH, NF - BLK), jnp.bfloat16)], axis=2)

    def per_station(carry, entry):
        signal, wave, shift_row, active_flag = entry
        frames = framed(signal, blocks)
        spectrum = jnp.dot(frames.reshape(CH * blocks, NF), data_table, preferred_element_type=jnp.float32)
        spectrum = spectrum.astype(jnp.bfloat16).reshape(CH, blocks, 2 * NF).astype(jnp.float32)
        weighted = station_spectrum(wave, shift_row, active_flag, tmpl_table, NF).astype(jnp.float32)
        x_real = spectrum[..., :NF]
        x_imag = spectrum[..., NF:]
        g_real = weighted[..., :NF]
        g_imag = weighted[..., NF:]
        total_real = carry[0] + jnp.einsum("tcf,cnf->tnf", g_real, x_real) - jnp.einsum("tcf,cnf->tnf", g_imag, x_imag)
        total_imag = carry[1] + jnp.einsum("tcf,cnf->tnf", g_real, x_imag) + jnp.einsum("tcf,cnf->tnf", g_imag, x_real)
        return (total_real, total_imag), None

    start = (jnp.zeros((TPL, blocks, NF), jnp.float32), jnp.zeros((TPL, blocks, NF), jnp.float32))
    totals, _ = lax.scan(per_station, start, (padded, templates, moveout, active))
    combined = jnp.concatenate([totals[0], totals[1]], axis=-1).reshape(TPL * blocks, 2 * NF)
    stack = jnp.dot(combined, inverse_table(NF, BLK), precision=lax.Precision.HIGHEST, preferred_element_type=jnp.float32)
    return stack.reshape(TPL, TIME)
```

```python
import jax
import jax.numpy as jnp
from jax import lax
from jax.experimental import pallas as pl
from jax.experimental.pallas import tpu as pltpu
from jax.sharding import PartitionSpec as P

XS, ZH = 4, 4
YS, ZL, CORES = 4, 4, 2
CH = 3
L = 256
NF = 512
BLK = 128
TPL = 32
LANES = 128
SUB = 8
MESH = pl.DeviceIdType.MESH


def gather_kernel(seis_ref, wave_ref, xs_ref, tg_ref, send_sem, recv_sem, local_sem):
    tm = lax.axis_index("tm")
    x, zh = tm // ZH, tm % ZH
    quarter = (seis_ref.shape[1] - NF) // XS
    span = xs_ref.shape[2]

    def segment(px):
        return seis_ref.at[:, pl.ds(pl.multiple_of(px * quarter, LANES), span)]

    peers = [(x + d) % XS for d in range(1, XS)]
    barrier = pltpu.get_barrier_semaphore()
    for px in peers:
        pl.semaphore_signal(barrier, inc=1, device_id={"tm": px * ZH + zh}, device_id_type=MESH)
    pl.semaphore_wait(barrier, XS - 1)
    copies = []
    for d, px in enumerate(peers):
        target = {"tm": px * ZH + zh}
        copies.append(pltpu.make_async_remote_copy(
            src_ref=wave_ref, dst_ref=tg_ref.at[x], send_sem=send_sem.at[0, d],
            recv_sem=recv_sem.at[0, d], device_id=target, device_id_type=MESH))
        copies.append(pltpu.make_async_remote_copy(
            src_ref=segment(px), dst_ref=xs_ref.at[x], send_sem=send_sem.at[1, d],
            recv_sem=recv_sem.at[1, d], device_id=target, device_id_type=MESH))
    copies.append(pltpu.make_async_copy(wave_ref, tg_ref.at[x], local_sem.at[0]))
    copies.append(pltpu.make_async_copy(segment(x), xs_ref.at[x], local_sem.at[1]))
    for copy in copies:
        copy.start()
    for copy in copies:
        copy.wait()


def correlate_kernel(shift_ref, active_ref, tg_ref, xs_ref, out_ref, rows_ref, moved_ref, w_ref, f_ref):
    zh = lax.axis_index("tm") % ZH
    nrows = xs_ref.shape[2] // LANES
    out_ref[...] = jnp.zeros_like(out_ref)

    def station(s, carry):
        scale = active_ref[s * ZH + zh].astype(jnp.float32)
        signal = xs_ref[s].astype(jnp.float32) * scale
        for c in range(CH):
            for r in range(nrows):
                rows_ref[c, r : r + 1, :] = signal[c : c + 1, r * LANES : (r + 1) * LANES]
        for t in range(TPL):
            wave = tg_ref[s, t].astype(jnp.float32)
            wide = jnp.concatenate([wave, jnp.zeros((CH, NF - L), jnp.float32)], axis=1)
            moved_ref[t, 0:CH, :] = pltpu.roll(wide, shift_ref[s * ZH + zh, t], 1)
        for c in range(CH):
            frames = jnp.concatenate([rows_ref[c, u : u + 32, :] for u in range(NF // BLK)], axis=1)
            for j in range(0, 16, 2):
                even = frames if j == 0 else pltpu.roll(frames, NF - SUB * j, 1)
                odd = pltpu.roll(frames, NF - SUB * (j + 1), 1)
                for z in range(ZH):
                    top = z * LANES + SUB * j
                    both = jnp.concatenate(
                        [even[SUB * z : SUB * z + SUB], odd[SUB * z : SUB * z + SUB]], axis=0)
                    f_ref[top : top + 2 * SUB, :] = both.astype(jnp.bfloat16)
            for block in range(0, TPL, 2):
                pair = []
                for at in (block, block + 1):
                    t = (at % 16) * 2 + at // 16
                    wide = jnp.broadcast_to(moved_ref[t, c : c + 1, :], (SUB, NF))
                    pair.append(pltpu.roll(wide, 0, 1, stride=1, stride_axis=0))
                w_ref[block * SUB : (block + 2) * SUB, :] = jnp.concatenate(
                    pair, axis=0).astype(jnp.bfloat16)
            out_ref[...] += lax.dot_general(
                w_ref[...], f_ref[...], (((1,), (1,)), ((), ())),
                preferred_element_type=jnp.float32)
        return carry

    lax.fori_loop(0, XS, station, 0)


def reduce_kernel(part_ref, out_ref, half_ref, near_ref, sum_ref, plane_ref, far_ref,
                  s1, r1, s2, r2, s3, r3):
    tm, tmpl = lax.axis_index("tm"), lax.axis_index("tmpl")
    x, zh = tm // ZH, tm % ZH
    y, zl, core = tmpl // (ZL * CORES), (tmpl // CORES) % ZL, tmpl % CORES
    half = part_ref.shape[0] // CORES
    block = half // YS

    def place(py, pzl, pcore, pzh):
        return {"tm": x * ZH + pzh, "tmpl": py * (ZL * CORES) + pzl * CORES + pcore}

    other = place(y, zl, 1 - core, zh)
    ys = [((y + d) % YS, place((y + d) % YS, zl, core, zh)) for d in range(1, YS)]
    zs = []
    for d in range(1, ZL * ZH):
        pzl, pzh = (zl + d % ZL) % ZL, (zh + d // ZL) % ZH
        zs.append((pzl, pzh, place(y, pzl, core, pzh)))
    barrier = pltpu.get_barrier_semaphore()
    for target in [other] + [p[-1] for p in ys] + [p[-1] for p in zs]:
        pl.semaphore_signal(barrier, inc=1, device_id=target, device_id_type=MESH)
    pl.semaphore_wait(barrier, 1 + len(ys) + len(zs))

    first = pltpu.make_async_remote_copy(
        src_ref=part_ref.at[pl.ds(pl.multiple_of((1 - core) * half, SUB), half)], dst_ref=half_ref,
        send_sem=s1, recv_sem=r1, device_id=other, device_id_type=MESH)
    first.start()
    first.wait()
    sum_ref[...] = part_ref[pl.ds(pl.multiple_of(core * half, SUB), half)] + half_ref[...]

    second = [
        pltpu.make_async_remote_copy(
            src_ref=sum_ref.at[pl.ds(pl.multiple_of(py * block, SUB), block)],
            dst_ref=near_ref.at[d], send_sem=s2.at[d], recv_sem=r2.at[d],
            device_id=target, device_id_type=MESH)
        for d, (py, target) in enumerate(ys)]
    for copy in second:
        copy.start()
    for copy in second:
        copy.wait()
    plane_ref[...] = (sum_ref[pl.ds(pl.multiple_of(y * block, SUB), block)]
                      + near_ref[0] + near_ref[1] + near_ref[2])

    def tile(pzl, pzh):
        return (pl.ds(pl.multiple_of(pzl * SUB, SUB), SUB),
                pl.ds(pl.multiple_of(pzh * LANES, LANES), LANES))

    third = [
        pltpu.make_async_remote_copy(
            src_ref=plane_ref.at[tile(pzl, pzh)], dst_ref=far_ref.at[d],
            send_sem=s3.at[d], recv_sem=r3.at[d], device_id=target, device_id_type=MESH)
        for d, (pzl, pzh, target) in enumerate(zs)]
    for copy in third:
        copy.start()
    for copy in third:
        copy.wait()
    total = plane_ref[tile(zl, zh)]
    for d in range(len(zs)):
        total = total + far_ref[d]
    out_ref[...] = total


def vmem(count):
    return [pl.BlockSpec(memory_space=pltpu.VMEM)] * count


def per_device(seismic, templates, moveout, active):
    window = seismic.shape[2]
    span = window // XS + NF
    padded = jnp.pad(seismic[0], ((0, 0), (0, NF)))
    dma = pltpu.SemaphoreType.DMA
    xs, tg = pl.pallas_call(
        gather_kernel,
        out_shape=(jax.ShapeDtypeStruct((XS, CH, span), jnp.bfloat16),
                   jax.ShapeDtypeStruct((XS, TPL, CH, L), jnp.bfloat16)),
        in_specs=vmem(2), out_specs=tuple(vmem(2)),
        scratch_shapes=[dma((2, XS - 1)), dma((2, XS - 1)), dma((2,))],
        compiler_params=pltpu.CompilerParams(collective_id=0, has_side_effects=True),
        name="gather_x",
    )(padded, templates[0])

    rows, columns = TPL * SUB, window // XS // SUB
    part = pl.pallas_call(
        correlate_kernel,
        out_shape=jax.ShapeDtypeStruct((rows, columns), jnp.float32),
        in_specs=[pl.BlockSpec(memory_space=pltpu.SMEM)] * 2 + vmem(2),
        out_specs=vmem(1)[0],
        scratch_shapes=[pltpu.VMEM((CH, 40, LANES), jnp.float32),
                        pltpu.VMEM((TPL, SUB, NF), jnp.float32),
                        pltpu.VMEM((rows, NF), jnp.bfloat16),
                        pltpu.VMEM((columns, NF), jnp.bfloat16)],
        name="correlate",
    )(moveout, active, tg, xs)

    half = rows // CORES
    block = half // YS
    others = ZL * ZH - 1
    tile = pl.pallas_call(
        reduce_kernel,
        out_shape=jax.ShapeDtypeStruct((SUB, LANES), jnp.float32),
        in_specs=vmem(1), out_specs=vmem(1)[0],
        scratch_shapes=[pltpu.VMEM((half, columns), jnp.float32),
                        pltpu.VMEM((YS - 1, block, columns), jnp.float32),
                        pltpu.VMEM((half, columns), jnp.float32),
                        pltpu.VMEM((block, columns), jnp.float32),
                        pltpu.VMEM((others, SUB, LANES), jnp.float32),
                        dma, dma, dma((YS - 1,)), dma((YS - 1,)), dma((others,)), dma((others,))],
        compiler_params=pltpu.CompilerParams(collective_id=1, has_side_effects=True),
        name="reduce_scatter",
    )(part)
    return tile.reshape(SUB, LANES // SUB, SUB).transpose(2, 1, 0).reshape(1, SUB * LANES)


def solution(mesh):
    in_specs = (
        P(("tmpl", "tm"), None, None),
        P(("tmpl", "tm"), None, None, None),
        P("tmpl", None),
        P("tmpl"),
    )
    out_specs = P("tmpl", "tm")
    return jax.shard_map(
        per_device, mesh=mesh, in_specs=in_specs, out_specs=out_specs, check_vma=False
    )
```

```python
import jax
import jax.numpy as jnp
from jax import lax
from jax.experimental import pallas as pl
from jax.experimental.pallas import tpu as pltpu
from jax.sharding import PartitionSpec as P

XS, ZH = 4, 4
YS, ZL, CORES = 4, 4, 2
CH = 3
L = 256
NF = 512
BLK = 128
TPL = 32
LANES = 128
SUB = 8
MESH = pl.DeviceIdType.MESH


def gather_kernel(seis_ref, wave_ref, xs_ref, tg_ref, send_sem, recv_sem, local_sem):
    tm = lax.axis_index("tm")
    x, zh = tm // ZH, tm % ZH
    quarter = (seis_ref.shape[1] - NF) // XS
    span = xs_ref.shape[2]

    def segment(px):
        return seis_ref.at[:, pl.ds(pl.multiple_of(px * quarter, LANES), span)]

    peers = [(x + d) % XS for d in range(1, XS)]
    barrier = pltpu.get_barrier_semaphore()
    for px in peers:
        pl.semaphore_signal(barrier, inc=1, device_id={"tm": px * ZH + zh}, device_id_type=MESH)
    pl.semaphore_wait(barrier, XS - 1)
    copies = []
    for d, px in enumerate(peers):
        target = {"tm": px * ZH + zh}
        copies.append(pltpu.make_async_remote_copy(
            src_ref=wave_ref, dst_ref=tg_ref.at[x], send_sem=send_sem.at[0, d],
            recv_sem=recv_sem.at[0, d], device_id=target, device_id_type=MESH))
        copies.append(pltpu.make_async_remote_copy(
            src_ref=segment(px), dst_ref=xs_ref.at[x], send_sem=send_sem.at[1, d],
            recv_sem=recv_sem.at[1, d], device_id=target, device_id_type=MESH))
    copies.append(pltpu.make_async_copy(wave_ref, tg_ref.at[x], local_sem.at[0]))
    copies.append(pltpu.make_async_copy(segment(x), xs_ref.at[x], local_sem.at[1]))
    for copy in copies:
        copy.start()
    for copy in copies:
        copy.wait()


def transpose_groups(tile):
    row = lax.broadcasted_iota(jnp.int32, tile.shape, 0)
    lane = lax.broadcasted_iota(jnp.int32, tile.shape, 1)
    for bit in (1, 2, 4):
        below = pltpu.roll(pltpu.roll(tile, SUB - bit, 0), bit, 1)
        above = pltpu.roll(pltpu.roll(tile, bit, 0), LANES - bit, 1)
        low, left = (row & bit) == 0, (lane & bit) == 0
        tile = jnp.where(low == left, tile, jnp.where(low, below, above))
    return tile


def correlate_kernel(shift_ref, active_ref, tg_ref, xs_ref, out_ref,
                     rows_ref, moved_ref, w_ref, f_ref, acc_ref,
                     core_send, core_recv, sum_ref, y_send, y_recv, plane_ref, z_send, z_recv,
                     s1, r1, s2, r2, s3, r3):
    tm, tmpl = lax.axis_index("tm"), lax.axis_index("tmpl")
    x, zh = tm // ZH, tm % ZH
    y, zl, core = tmpl // (ZL * CORES), (tmpl // CORES) % ZL, tmpl % CORES
    nz = ZL * ZH
    z = zh * ZL + zl
    half = acc_ref.shape[1] // CORES
    block = half // YS

    def place(py, pz, pcore):
        return {"tm": x * ZH + pz // ZL, "tmpl": py * (ZL * CORES) + (pz % ZL) * CORES + pcore}

    other = place(y, z, 1 - core)
    ys = [(d - 1, (y + d) % YS) for d in (2, 1, 3)]
    zs = [(d - 1, (z + d) % nz) for d in sorted(range(1, nz), key=lambda d: abs(d - nz // 2))]
    barrier = pltpu.get_barrier_semaphore()
    targets = [place(y, pz, core) for _, pz in zs] + [place(py, z, core) for _, py in ys] + [other]
    for target in targets:
        pl.semaphore_signal(barrier, inc=1, device_id=target, device_id_type=MESH)

    acc_ref[...] = jnp.zeros_like(acc_ref)
    nrows = xs_ref.shape[2] // LANES

    def multiply(s, c, part):
        frames = jnp.concatenate(
            [rows_ref[s, c, u + 16 * part : u + 16 * part + 16, :] for u in range(NF // BLK)], axis=1)
        for j in range(0, 16, 2):
            even = frames if j == 0 else pltpu.roll(frames, NF - SUB * j, 1)
            odd = pltpu.roll(frames, NF - SUB * (j + 1), 1)
            for k in range(2):
                top = k * LANES + SUB * j
                both = jnp.concatenate(
                    [even[SUB * k : SUB * k + SUB], odd[SUB * k : SUB * k + SUB]], axis=0)
                f_ref[top : top + 2 * SUB, :] = both.astype(jnp.bfloat16)
        acc_ref[part] += lax.dot_general(
            w_ref[s, c], f_ref[...], (((1,), (1,)), ((), ())), preferred_element_type=jnp.float32)

    def early(s, carry):
        scale = active_ref[s * ZH + zh].astype(jnp.float32)
        signal = xs_ref[s].astype(jnp.float32) * scale
        for c in range(CH):
            for r in range(nrows):
                rows_ref[s, c, r : r + 1, :] = signal[c : c + 1, r * LANES : (r + 1) * LANES]
        for t in range(TPL):
            wave = tg_ref[s, t].astype(jnp.float32)
            wide = jnp.concatenate([wave, jnp.zeros((CH, NF - L), jnp.float32)], axis=1)
            moved_ref[t, 0:CH, :] = pltpu.roll(wide, shift_ref[s * ZH + zh, t], 1)
        for c in range(CH):
            for at in range(0, TPL, 2):
                pair = []
                for slot in (at, at + 1):
                    t = (slot % 16) * 2 + slot // 16
                    wide = jnp.broadcast_to(moved_ref[t, c : c + 1, :], (SUB, NF))
                    pair.append(pltpu.roll(wide, 0, 1, stride=1, stride_axis=0))
                w_ref[s, c, at * SUB : (at + 2) * SUB, :] = jnp.concatenate(
                    pair, axis=0).astype(jnp.bfloat16)
            multiply(s, c, 0)
        return carry

    def late(s, carry):
        for c in range(CH):
            multiply(s, c, 1)
        return carry

    away = pl.ds(pl.multiple_of((1 - core) * half, SUB), half)
    mine = pl.ds(pl.multiple_of(core * half, SUB), half)

    def to_core(part):
        return pltpu.make_async_remote_copy(
            src_ref=core_send.at[part], dst_ref=core_recv.at[part], send_sem=s1.at[part],
            recv_sem=r1.at[part], device_id=other, device_id_type=MESH)

    lax.fori_loop(0, XS, early, 0)
    core_send[0] = acc_ref[0, away].astype(jnp.bfloat16)
    pl.semaphore_wait(barrier, len(targets))
    to_core(0).start()
    lax.fori_loop(0, XS, late, 0)
    core_send[1] = acc_ref[1, away].astype(jnp.bfloat16)
    to_core(1).start()

    def to_y(part, d, py):
        return pltpu.make_async_remote_copy(
            src_ref=y_send.at[part, pl.ds(pl.multiple_of(py * block, block), block)],
            dst_ref=y_recv.at[part, d], send_sem=s2.at[part, d], recv_sem=r2.at[part, d],
            device_id=place(py, z, core), device_id_type=MESH)

    for part in range(2):
        to_core(part).wait()
        total = acc_ref[part, mine] + core_recv[part].astype(jnp.float32)
        sum_ref[part] = total
        y_send[part] = total.astype(jnp.bfloat16)
        for d, py in ys:
            to_y(part, d, py).start()

    for part in range(2):
        total = sum_ref[part, pl.ds(pl.multiple_of(y * block, block), block)]
        for d, py in ys:
            to_y(part, d, py).wait()
            total = total + y_recv[part, d].astype(jnp.float32)
        for pzl in range(ZL):
            for k in range(2):
                tile = total[pzl * SUB : (pzl + 1) * SUB, k * LANES : (k + 1) * LANES]
                at = (2 * part + k) * ZL + pzl
                plane_ref[at] = tile
                z_send[at] = tile.astype(jnp.bfloat16)

    last = [
        pltpu.make_async_remote_copy(
            src_ref=z_send.at[pz], dst_ref=z_recv.at[d], send_sem=s3.at[d], recv_sem=r3.at[d],
            device_id=place(y, pz, core), device_id_type=MESH)
        for d, pz in zs]
    for copy in last:
        copy.start()
    for copy in last:
        copy.wait()
    total = plane_ref[z]
    for d in range(nz - 1):
        total = total + z_recv[d].astype(jnp.float32)
    out_ref[...] = transpose_groups(total)


def vmem(count):
    return [pl.BlockSpec(memory_space=pltpu.VMEM)] * count


def per_device(seismic, templates, moveout, active):
    window = seismic.shape[2]
    span = window // XS + NF
    padded = jnp.pad(seismic[0], ((0, 0), (0, NF)))
    dma = pltpu.SemaphoreType.DMA
    xs, tg = pl.pallas_call(
        gather_kernel,
        out_shape=(jax.ShapeDtypeStruct((XS, CH, span), jnp.bfloat16),
                   jax.ShapeDtypeStruct((XS, TPL, CH, L), jnp.bfloat16)),
        in_specs=vmem(2), out_specs=tuple(vmem(2)),
        scratch_shapes=[dma((2, XS - 1)), dma((2, XS - 1)), dma((2,))],
        compiler_params=pltpu.CompilerParams(collective_id=0, has_side_effects=True),
        name="gather_x",
    )(padded, templates[0])

    rows, columns = TPL * SUB, window // XS // SUB // 2
    half = rows // CORES
    block = half // YS
    devices = ZL * ZH
    bf16, f32 = jnp.bfloat16, jnp.float32
    tile = pl.pallas_call(
        correlate_kernel,
        out_shape=jax.ShapeDtypeStruct((SUB, LANES), f32),
        in_specs=[pl.BlockSpec(memory_space=pltpu.SMEM)] * 2 + vmem(2),
        out_specs=vmem(1)[0],
        scratch_shapes=[pltpu.VMEM((XS, CH, 40, LANES), f32),
                        pltpu.VMEM((TPL, SUB, NF), f32),
                        pltpu.VMEM((XS, CH, rows, NF), bf16),
                        pltpu.VMEM((columns, NF), bf16),
                        pltpu.VMEM((2, rows, columns), f32),
                        pltpu.VMEM((2, half, columns), bf16),
                        pltpu.VMEM((2, half, columns), bf16),
                        pltpu.VMEM((2, half, columns), f32),
                        pltpu.VMEM((2, half, columns), bf16),
                        pltpu.VMEM((2, YS - 1, block, columns), bf16),
                        pltpu.VMEM((devices, SUB, LANES), f32),
                        pltpu.VMEM((devices, SUB, LANES), bf16),
                        pltpu.VMEM((devices - 1, SUB, LANES), bf16),
                        dma((2,)), dma((2,)), dma((2, YS - 1)), dma((2, YS - 1)),
                        dma((devices - 1,)), dma((devices - 1,))],
        compiler_params=pltpu.CompilerParams(collective_id=1, has_side_effects=True),
        name="correlate_reduce",
    )(moveout, active, tg, xs)
    return tile.reshape(1, SUB * LANES)


def solution(mesh):
    in_specs = (
        P(("tmpl", "tm"), None, None),
        P(("tmpl", "tm"), None, None, None),
        P("tmpl", None),
        P("tmpl"),
    )
    out_specs = P("tmpl", "tm")
    return jax.shard_map(
        per_device, mesh=mesh, in_specs=in_specs, out_specs=out_specs, check_vma=False
    )
```

```python
import jax
import jax.numpy as jnp
from jax import lax
from jax.experimental import pallas as pl
from jax.experimental.pallas import tpu as pltpu
from jax.sharding import PartitionSpec as P

XS, ZH = 4, 4
YS, ZL, CORES = 4, 4, 2
CH = 3
L = 256
NF = 512
BLK = 128
TPL = 32
LANES = 128
SUB = 8
MESH = pl.DeviceIdType.MESH


def transpose_groups(tile):
    row = lax.broadcasted_iota(jnp.int32, tile.shape, 0)
    lane = lax.broadcasted_iota(jnp.int32, tile.shape, 1)
    for bit in (1, 2, 4):
        below = pltpu.roll(pltpu.roll(tile, SUB - bit, 0), bit, 1)
        above = pltpu.roll(pltpu.roll(tile, bit, 0), LANES - bit, 1)
        low, left = (row & bit) == 0, (lane & bit) == 0
        tile = jnp.where(low == left, tile, jnp.where(low, below, above))
    return tile


def stack_kernel(shift_ref, active_ref, seis_ref, wave_ref, out_ref,
                 xs_ref, tg_ref, gs, gr, gl, rows_ref, moved_ref, w_ref, f_ref, acc_ref,
                 core_send, core_recv, sum_ref, y_send, y_recv, plane_ref, z_send, z_recv,
                 s1, r1, s2, r2, s3, r3):
    tm, tmpl = lax.axis_index("tm"), lax.axis_index("tmpl")
    x, zh = tm // ZH, tm % ZH
    y, zl, core = tmpl // (ZL * CORES), (tmpl // CORES) % ZL, tmpl % CORES
    nz = ZL * ZH
    z = zh * ZL + zl
    half = acc_ref.shape[1] // CORES
    block = half // YS

    quarter = seis_ref.shape[1] // XS
    halo = xs_ref.shape[2] - quarter

    def along_x(px):
        return {"tm": px * ZH + zh}

    def pieces(px):
        follow = (px + 1) % XS * quarter
        return [
            (seis_ref.at[:, pl.ds(pl.multiple_of(px * quarter, LANES), quarter)],
             xs_ref.at[x, :, 0:quarter]),
            (seis_ref.at[:, pl.ds(pl.multiple_of(follow, LANES), halo)],
             xs_ref.at[x, :, quarter : quarter + halo])]

    def send(kind, source, target, d, back):
        return pltpu.make_async_remote_copy(
            src_ref=source, dst_ref=target, send_sem=gs.at[kind, d], recv_sem=gr.at[kind, back],
            device_id=along_x((x + d) % XS), device_id_type=MESH)

    def place(py, pz, pcore):
        return {"tm": x * ZH + pz // ZL, "tmpl": py * (ZL * CORES) + (pz % ZL) * CORES + pcore}

    other = place(y, z, 1 - core)
    ys = [(d - 1, (y + d) % YS) for d in (2, 1, 3)]
    zs = [(d - 1, (z + d) % nz) for d in sorted(range(1, nz), key=lambda d: abs(d - nz // 2))]
    barrier = pltpu.get_barrier_semaphore()
    targets = [place(y, pz, core) for _, pz in zs] + [place(py, z, core) for _, py in ys] + [other]
    targets += [along_x((x + d) % XS) for d in range(1, XS)]
    for target in targets:
        pl.semaphore_signal(barrier, inc=1, device_id=target, device_id_type=MESH)

    local = [pltpu.make_async_copy(wave_ref, tg_ref.at[x], gl.at[0])]
    local += [pltpu.make_async_copy(*pair, gl.at[1 + k]) for k, pair in enumerate(pieces(x))]
    for copy in local:
        copy.start()
    acc_ref[...] = jnp.zeros_like(acc_ref)
    for copy in local:
        copy.wait()
    nrows = xs_ref.shape[2] // LANES

    def multiply(s, c, part):
        frames = jnp.concatenate(
            [rows_ref[s, c, u + 16 * part : u + 16 * part + 16, :] for u in range(NF // BLK)], axis=1)
        for j in range(0, 16, 2):
            even = frames if j == 0 else pltpu.roll(frames, NF - SUB * j, 1)
            odd = pltpu.roll(frames, NF - SUB * (j + 1), 1)
            for k in range(2):
                top = k * LANES + SUB * j
                both = jnp.concatenate(
                    [even[SUB * k : SUB * k + SUB], odd[SUB * k : SUB * k + SUB]], axis=0)
                f_ref[top : top + 2 * SUB, :] = both.astype(jnp.bfloat16)
        acc_ref[part] += lax.dot_general(
            w_ref[s, c], f_ref[...], (((1,), (1,)), ((), ())), preferred_element_type=jnp.float32)

    def early(s):
        scale = active_ref[s * ZH + zh].astype(jnp.float32)
        column = lax.broadcasted_iota(jnp.int32, xs_ref.shape[1:], 1)
        last_quarter = jnp.full(xs_ref.shape[1:], x, jnp.int32) == XS - 1
        past = jnp.logical_and(last_quarter, column >= quarter)
        signal = jnp.where(past, 0.0, xs_ref[s].astype(jnp.float32) * scale)
        for c in range(CH):
            for r in range(nrows):
                rows_ref[s, c, r : r + 1, :] = signal[c : c + 1, r * LANES : (r + 1) * LANES]
        waves = [tg_ref[s, c].astype(jnp.float32) for c in range(CH)]
        for t in range(TPL):
            wave = jnp.concatenate([w[t : t + 1] for w in waves], axis=0)
            wide = jnp.concatenate([wave, jnp.zeros((CH, NF - L), jnp.float32)], axis=1)
            moved_ref[t, 0:CH, :] = pltpu.roll(wide, shift_ref[s * ZH + zh, t], 1)
        for c in range(CH):
            for at in range(0, TPL, 2):
                pair = []
                for slot in (at, at + 1):
                    t = (slot % 16) * 2 + slot // 16
                    wide = jnp.broadcast_to(moved_ref[t, c : c + 1, :], (SUB, NF))
                    pair.append(pltpu.roll(wide, 0, 1, stride=1, stride_axis=0))
                w_ref[s, c, at * SUB : (at + 2) * SUB, :] = jnp.concatenate(
                    pair, axis=0).astype(jnp.bfloat16)
            multiply(s, c, 0)

    def late(s, carry):
        for c in range(CH):
            multiply(s, c, 1)
        return carry

    away = pl.ds(pl.multiple_of((1 - core) * half, SUB), half)
    mine = pl.ds(pl.multiple_of(core * half, SUB), half)

    def to_core(part):
        return pltpu.make_async_remote_copy(
            src_ref=core_send.at[part], dst_ref=core_recv.at[part], send_sem=s1.at[part],
            recv_sem=r1.at[part], device_id=other, device_id_type=MESH)

    def to_y(part, d, py):
        return pltpu.make_async_remote_copy(
            src_ref=y_send.at[part, pl.ds(pl.multiple_of(py * block, block), block)],
            dst_ref=y_recv.at[part, d], send_sem=s2.at[part, d], recv_sem=r2.at[part, d],
            device_id=place(py, z, core), device_id_type=MESH)

    def after_core(part):
        to_core(part).wait()
        total = acc_ref[part, mine] + core_recv[part].astype(jnp.float32)
        sum_ref[part] = total
        y_send[part] = total.astype(jnp.bfloat16)
        for d, py in ys:
            to_y(part, d, py).start()

    gather = []
    for d in (1, 3):
        gather.append(send(0, wave_ref, tg_ref.at[x], d, XS - d))
    for d in (1, 3, 2):
        for k, (source, target) in enumerate(pieces((x + d) % XS)):
            gather.append(send(1 + k, source, target, d, XS - d))
    onward = tg_ref.at[(x + 1) % XS]
    relay = pltpu.make_async_remote_copy(
        src_ref=onward, dst_ref=onward, send_sem=gs.at[0, 2], recv_sem=gr.at[0, 2],
        device_id=along_x((x + 3) % XS), device_id_type=MESH)
    pl.semaphore_wait(barrier, len(targets))
    for copy in gather:
        copy.start()

    def arrive(step, carry):
        offset = step ^ (step // 2)
        s = (x + offset) % XS

        @pl.when(step > 0)
        def _():
            send(0, wave_ref, tg_ref.at[s], 1, offset).wait_recv()

            @pl.when(step == 1)
            def _():
                relay.start()

            for k, (source, _) in enumerate(pieces(x)):
                target = xs_ref.at[s, :, k * quarter : k * quarter + source.shape[1]]
                send(1 + k, source, target, 1, offset).wait_recv()

        early(s)
        return carry

    lax.fori_loop(0, XS, arrive, 0)
    for copy in gather + [relay]:
        copy.wait_send()
    core_send[0] = acc_ref[0, away].astype(jnp.bfloat16)
    to_core(0).start()
    lax.fori_loop(0, 2, late, 0)
    after_core(0)
    lax.fori_loop(2, XS, late, 0)
    core_send[1] = acc_ref[1, away].astype(jnp.bfloat16)
    to_core(1).start()
    after_core(1)

    for part in range(2):
        total = sum_ref[part, pl.ds(pl.multiple_of(y * block, block), block)]
        for d, py in ys:
            to_y(part, d, py).wait()
            total = total + y_recv[part, d].astype(jnp.float32)
        for pzl in range(ZL):
            for k in range(2):
                tile = total[pzl * SUB : (pzl + 1) * SUB, k * LANES : (k + 1) * LANES]
                at = (2 * part + k) * ZL + pzl
                plane_ref[at] = tile
                z_send[at] = tile.astype(jnp.bfloat16)

    last = [
        pltpu.make_async_remote_copy(
            src_ref=z_send.at[pz], dst_ref=z_recv.at[d], send_sem=s3.at[d], recv_sem=r3.at[d],
            device_id=place(y, pz, core), device_id_type=MESH)
        for d, pz in zs]
    for copy in last:
        copy.start()
    for copy in last:
        copy.wait()
    total = plane_ref[z]
    for d in range(nz - 1):
        total = total + z_recv[d].astype(jnp.float32)
    out_ref[...] = transpose_groups(total)


def vmem(count):
    return [pl.BlockSpec(memory_space=pltpu.VMEM)] * count


def per_device(seismic, templates, moveout, active):
    window = seismic.shape[2]
    span = window // XS + NF
    dma = pltpu.SemaphoreType.DMA
    rows, columns = TPL * SUB, window // XS // SUB // 2
    half = rows // CORES
    block = half // YS
    devices = ZL * ZH
    bf16, f32 = jnp.bfloat16, jnp.float32
    tile = pl.pallas_call(
        stack_kernel,
        out_shape=jax.ShapeDtypeStruct((SUB, LANES), f32),
        in_specs=[pl.BlockSpec(memory_space=pltpu.SMEM)] * 2 + vmem(2),
        out_specs=vmem(1)[0],
        scratch_shapes=[pltpu.VMEM((XS, CH, span), bf16),
                        pltpu.VMEM((XS, CH, TPL, L), bf16),
                        dma((3, XS)), dma((3, XS)), dma((3,)),
                        pltpu.VMEM((XS, CH, 40, LANES), f32),
                        pltpu.VMEM((TPL, SUB, NF), f32),
                        pltpu.VMEM((XS, CH, rows, NF), bf16),
                        pltpu.VMEM((columns, NF), bf16),
                        pltpu.VMEM((2, rows, columns), f32),
                        pltpu.VMEM((2, half, columns), bf16),
                        pltpu.VMEM((2, half, columns), bf16),
                        pltpu.VMEM((2, half, columns), f32),
                        pltpu.VMEM((2, half, columns), bf16),
                        pltpu.VMEM((2, YS - 1, block, columns), bf16),
                        pltpu.VMEM((devices, SUB, LANES), f32),
                        pltpu.VMEM((devices, SUB, LANES), bf16),
                        pltpu.VMEM((devices - 1, SUB, LANES), bf16),
                        dma((2,)), dma((2,)), dma((2, YS - 1)), dma((2, YS - 1)),
                        dma((devices - 1,)), dma((devices - 1,))],
        compiler_params=pltpu.CompilerParams(collective_id=0, has_side_effects=True),
        name="stack",
    )(moveout, active, seismic[0], templates[0].transpose(1, 0, 2))
    return tile.reshape(1, SUB * LANES)


def solution(mesh):
    in_specs = (
        P(("tmpl", "tm"), None, None),
        P(("tmpl", "tm"), None, None, None),
        P("tmpl", None),
        P("tmpl"),
    )
    out_specs = P("tmpl", "tm")
    return jax.shard_map(
        per_device, mesh=mesh, in_specs=in_specs, out_specs=out_specs, check_vma=False
    )
```

```python
import jax
import jax.numpy as jnp
from jax import lax
from jax.experimental import pallas as pl
from jax.experimental.pallas import tpu as pltpu
from jax.sharding import PartitionSpec as P

XS, ZH = 4, 4
YS, ZL, CORES = 4, 4, 2
CH = 3
L = 256
NF = 512
BLK = 128
TPL = 32
LANES = 128
SUB = 8
MESH = pl.DeviceIdType.MESH


def transpose_groups(tile):
    row = lax.broadcasted_iota(jnp.int32, tile.shape, 0)
    lane = lax.broadcasted_iota(jnp.int32, tile.shape, 1)
    for bit in (1, 2, 4):
        below = pltpu.roll(pltpu.roll(tile, SUB - bit, 0), bit, 1)
        above = pltpu.roll(pltpu.roll(tile, bit, 0), LANES - bit, 1)
        low, left = (row & bit) == 0, (lane & bit) == 0
        tile = jnp.where(low == left, tile, jnp.where(low, below, above))
    return tile


def stack_kernel(shift_ref, active_ref, seis_ref, wave_ref, out_ref,
                 xs_ref, tg_ref, gs, gr, gl, rows_ref, moved_ref, w_ref, f_ref, acc_ref,
                 core_send, core_recv, sum_ref, y_send, y_recv, plane_ref, z_send, z_recv,
                 s1, r1, s2, r2, s3, r3, ready):
    tm, tmpl = lax.axis_index("tm"), lax.axis_index("tmpl")
    x, zh = tm // ZH, tm % ZH
    y, zl, core = tmpl // (ZL * CORES), (tmpl // CORES) % ZL, tmpl % CORES
    nz = ZL * ZH
    z = zh * ZL + zl
    half = acc_ref.shape[1] // CORES
    block = half // YS

    quarter = seis_ref.shape[1] // XS
    halo = xs_ref.shape[2] - quarter

    def along_x(px):
        return {"tm": px * ZH + zh}

    def pieces(px):
        follow = (px + 1) % XS * quarter
        return [
            (seis_ref.at[:, pl.ds(pl.multiple_of(px * quarter, LANES), quarter)],
             xs_ref.at[x, :, 0:quarter]),
            (seis_ref.at[:, pl.ds(pl.multiple_of(follow, LANES), halo)],
             xs_ref.at[x, :, quarter : quarter + halo])]

    def send(kind, source, target, d, back):
        return pltpu.make_async_remote_copy(
            src_ref=source, dst_ref=target, send_sem=gs.at[kind, d], recv_sem=gr.at[kind, back],
            device_id=along_x((x + d) % XS), device_id_type=MESH)

    def tell(reach):
        for d in (reach, nz - reach):
            pl.semaphore_signal(ready.at[reach // 2], inc=1, device_id=place(y, (z + d) % nz, core),
                                device_id_type=MESH)

    def heard(reach):
        pl.semaphore_wait(ready.at[reach // 2], 2)

    def place(py, pz, pcore):
        return {"tm": x * ZH + pz // ZL, "tmpl": py * (ZL * CORES) + (pz % ZL) * CORES + pcore}

    other = place(y, z, 1 - core)
    ys = [(d - 1, (y + d) % YS) for d in (2, 1, 3)]
    zs = [(d - 1, (z + d) % nz) for d in sorted(range(1, nz), key=lambda d: abs(d - nz // 2))]
    barrier = pltpu.get_barrier_semaphore()
    targets = [place(y, (z + d) % nz, core) for d in (1, nz - 1)]
    targets += [place(py, z, core) for _, py in ys] + [other]
    targets += [along_x((x + d) % XS) for d in range(1, XS)]
    for target in targets:
        pl.semaphore_signal(barrier, inc=1, device_id=target, device_id_type=MESH)

    local = [pltpu.make_async_copy(wave_ref, tg_ref.at[x], gl.at[0])]
    local += [pltpu.make_async_copy(*pair, gl.at[1 + k]) for k, pair in enumerate(pieces(x))]
    for copy in local:
        copy.start()
    acc_ref[...] = jnp.zeros_like(acc_ref)
    for copy in local:
        copy.wait()
    nrows = xs_ref.shape[2] // LANES

    def multiply(s, c, part):
        frames = jnp.concatenate(
            [rows_ref[s, c, u + 16 * part : u + 16 * part + 16, :] for u in range(NF // BLK)], axis=1)
        for j in range(0, 16, 2):
            even = frames if j == 0 else pltpu.roll(frames, NF - SUB * j, 1)
            odd = pltpu.roll(frames, NF - SUB * (j + 1), 1)
            for k in range(2):
                top = k * LANES + SUB * j
                both = jnp.concatenate(
                    [even[SUB * k : SUB * k + SUB], odd[SUB * k : SUB * k + SUB]], axis=0)
                f_ref[top : top + 2 * SUB, :] = both.astype(jnp.bfloat16)
        acc_ref[part] += lax.dot_general(
            w_ref[s, c], f_ref[...], (((1,), (1,)), ((), ())), preferred_element_type=jnp.float32)

    def early(s):
        scale = active_ref[s * ZH + zh].astype(jnp.float32)
        column = lax.broadcasted_iota(jnp.int32, xs_ref.shape[1:], 1)
        last_quarter = jnp.full(xs_ref.shape[1:], x, jnp.int32) == XS - 1
        past = jnp.logical_and(last_quarter, column >= quarter)
        signal = jnp.where(past, 0.0, xs_ref[s].astype(jnp.float32) * scale)
        for c in range(CH):
            for r in range(nrows):
                rows_ref[s, c, r : r + 1, :] = signal[c : c + 1, r * LANES : (r + 1) * LANES]
        waves = [tg_ref[s, c].astype(jnp.float32) for c in range(CH)]
        for t in range(TPL):
            wave = jnp.concatenate([w[t : t + 1] for w in waves], axis=0)
            wide = jnp.concatenate([wave, jnp.zeros((CH, NF - L), jnp.float32)], axis=1)
            moved_ref[t, 0:CH, :] = pltpu.roll(wide, shift_ref[s * ZH + zh, t], 1)
        for c in range(CH):
            for at in range(0, TPL, 2):
                pair = []
                for slot in (at, at + 1):
                    t = (slot % 16) * 2 + slot // 16
                    wide = jnp.broadcast_to(moved_ref[t, c : c + 1, :], (SUB, NF))
                    pair.append(pltpu.roll(wide, 0, 1, stride=1, stride_axis=0))
                w_ref[s, c, at * SUB : (at + 2) * SUB, :] = jnp.concatenate(
                    pair, axis=0).astype(jnp.bfloat16)
            multiply(s, c, 0)

    def late(s):
        for c in range(CH):
            multiply(s, c, 1)

    away = pl.ds(pl.multiple_of((1 - core) * half, SUB), half)
    mine = pl.ds(pl.multiple_of(core * half, SUB), half)

    def to_core(part):
        return pltpu.make_async_remote_copy(
            src_ref=core_send.at[part], dst_ref=core_recv.at[part], send_sem=s1.at[part],
            recv_sem=r1.at[part], device_id=other, device_id_type=MESH)

    def to_y(part, d, py):
        return pltpu.make_async_remote_copy(
            src_ref=y_send.at[part, pl.ds(pl.multiple_of(py * block, block), block)],
            dst_ref=y_recv.at[part, d], send_sem=s2.at[part, d], recv_sem=r2.at[part, d],
            device_id=place(py, z, core), device_id_type=MESH)

    def after_core(part):
        to_core(part).wait()
        total = acc_ref[part, mine] + core_recv[part].astype(jnp.float32)
        sum_ref[part] = total
        y_send[part] = total.astype(jnp.bfloat16)
        for d, py in ys:
            to_y(part, d, py).start()

    gather = []
    for d in (1, 3):
        gather.append(send(0, wave_ref, tg_ref.at[x], d, XS - d))
    for d in (1, 3, 2):
        for k, (source, target) in enumerate(pieces((x + d) % XS)):
            gather.append(send(1 + k, source, target, d, XS - d))
    onward = tg_ref.at[(x + 1) % XS]
    relay = pltpu.make_async_remote_copy(
        src_ref=onward, dst_ref=onward, send_sem=gs.at[0, 2], recv_sem=gr.at[0, 2],
        device_id=along_x((x + 3) % XS), device_id_type=MESH)
    pl.semaphore_wait(barrier, len(targets))
    for copy in gather:
        copy.start()
    tell(1)

    def arrive(step, carry):
        offset = step ^ (step // 2)
        s = (x + offset) % XS

        @pl.when(step > 0)
        def _():
            send(0, wave_ref, tg_ref.at[s], 1, offset).wait_recv()

            @pl.when(step == 1)
            def _():
                relay.start()

            for k, (source, _) in enumerate(pieces(x)):
                target = xs_ref.at[s, :, k * quarter : k * quarter + source.shape[1]]
                send(1 + k, source, target, 1, offset).wait_recv()

        @pl.when(step == 1)
        def _():
            heard(1)
            tell(2)

        @pl.when(step == 2)
        def _():
            heard(2)
            tell(4)

        early(s)

        @pl.when(step < XS - 1)
        def _():
            late(s)

        return carry

    lax.fori_loop(0, XS, arrive, 0)
    core_send[0] = acc_ref[0, away].astype(jnp.bfloat16)
    to_core(0).start()
    late((x + 2) % XS)
    core_send[1] = acc_ref[1, away].astype(jnp.bfloat16)
    to_core(1).start()
    after_core(0)
    after_core(1)
    for copy in gather + [relay]:
        copy.wait_send()

    for part in range(2):
        total = sum_ref[part, pl.ds(pl.multiple_of(y * block, block), block)]
        for d, py in ys:
            to_y(part, d, py).wait()
            total = total + y_recv[part, d].astype(jnp.float32)
        for pzl in range(ZL):
            for k in range(2):
                tile = total[pzl * SUB : (pzl + 1) * SUB, k * LANES : (k + 1) * LANES]
                at = (2 * part + k) * ZL + pzl
                plane_ref[at] = tile
                z_send[at] = tile.astype(jnp.bfloat16)

    last = [
        pltpu.make_async_remote_copy(
            src_ref=z_send.at[pz], dst_ref=z_recv.at[d], send_sem=s3.at[d], recv_sem=r3.at[d],
            device_id=place(y, pz, core), device_id_type=MESH)
        for d, pz in zs]
    heard(4)
    for copy in last:
        copy.start()
    for copy in last:
        copy.wait()
    total = plane_ref[z]
    for d in range(nz - 1):
        total = total + z_recv[d].astype(jnp.float32)
    out_ref[...] = transpose_groups(total)


def vmem(count):
    return [pl.BlockSpec(memory_space=pltpu.VMEM)] * count


def per_device(seismic, templates, moveout, active):
    window = seismic.shape[2]
    span = window // XS + NF
    dma = pltpu.SemaphoreType.DMA
    rows, columns = TPL * SUB, window // XS // SUB // 2
    half = rows // CORES
    block = half // YS
    devices = ZL * ZH
    bf16, f32 = jnp.bfloat16, jnp.float32
    tile = pl.pallas_call(
        stack_kernel,
        out_shape=jax.ShapeDtypeStruct((SUB, LANES), f32),
        in_specs=[pl.BlockSpec(memory_space=pltpu.SMEM)] * 2 + vmem(2),
        out_specs=vmem(1)[0],
        scratch_shapes=[pltpu.VMEM((XS, CH, span), bf16),
                        pltpu.VMEM((XS, CH, TPL, L), bf16),
                        dma((3, XS)), dma((3, XS)), dma((3,)),
                        pltpu.VMEM((XS, CH, 40, LANES), f32),
                        pltpu.VMEM((TPL, SUB, NF), f32),
                        pltpu.VMEM((XS, CH, rows, NF), bf16),
                        pltpu.VMEM((columns, NF), bf16),
                        pltpu.VMEM((2, rows, columns), f32),
                        pltpu.VMEM((2, half, columns), bf16),
                        pltpu.VMEM((2, half, columns), bf16),
                        pltpu.VMEM((2, half, columns), f32),
                        pltpu.VMEM((2, half, columns), bf16),
                        pltpu.VMEM((2, YS - 1, block, columns), bf16),
                        pltpu.VMEM((devices, SUB, LANES), f32),
                        pltpu.VMEM((devices, SUB, LANES), bf16),
                        pltpu.VMEM((devices - 1, SUB, LANES), bf16),
                        dma((2,)), dma((2,)), dma((2, YS - 1)), dma((2, YS - 1)),
                        dma((devices - 1,)), dma((devices - 1,)),
                        pltpu.SemaphoreType.REGULAR((3,))],
        compiler_params=pltpu.CompilerParams(collective_id=0, has_side_effects=True),
        name="stack",
    )(moveout, active, seismic[0], templates[0].transpose(1, 0, 2))
    return tile.reshape(1, SUB * LANES)


def solution(mesh):
    in_specs = (
        P(("tmpl", "tm"), None, None),
        P(("tmpl", "tm"), None, None, None),
        P("tmpl", None),
        P("tmpl"),
    )
    out_specs = P("tmpl", "tm")
    return jax.shard_map(
        per_device, mesh=mesh, in_specs=in_specs, out_specs=out_specs, check_vma=False
    )
```

```python
import jax
import jax.numpy as jnp
from jax import lax
from jax.experimental import pallas as pl
from jax.experimental.pallas import tpu as pltpu
from jax.sharding import PartitionSpec as P

XS, ZH = 4, 4
YS, ZL, CORES = 4, 4, 2
CH = 3
L = 256
NF = 512
BLK = 128
TPL = 32
LANES = 128
SUB = 8
MESH = pl.DeviceIdType.MESH


def transpose_groups(tile):
    row = lax.broadcasted_iota(jnp.int32, tile.shape, 0)
    lane = lax.broadcasted_iota(jnp.int32, tile.shape, 1)
    for bit in (1, 2, 4):
        below = pltpu.roll(pltpu.roll(tile, SUB - bit, 0), bit, 1)
        above = pltpu.roll(pltpu.roll(tile, bit, 0), LANES - bit, 1)
        low, left = (row & bit) == 0, (lane & bit) == 0
        tile = jnp.where(low == left, tile, jnp.where(low, below, above))
    return tile


def stack_kernel(shift_hbm, active_hbm, seis_ref, wave_ref, out_ref,
                 shift_ref, active_ref, xs_ref, tg_ref, gs, gr, gl, rows_ref, moved_ref, w_ref, f_ref, acc_ref,
                 core_send, core_recv, sum_ref, y_send, y_recv, plane_ref, z_send, z_recv,
                 s1, r1, s2, r2, s3, r3, ready):
    tm, tmpl = lax.axis_index("tm"), lax.axis_index("tmpl")
    x, zh = tm // ZH, tm % ZH
    y, zl, core = tmpl // (ZL * CORES), (tmpl // CORES) % ZL, tmpl % CORES
    nz = ZL * ZH
    z = zh * ZL + zl
    half = acc_ref.shape[1] // CORES
    block = half // YS

    quarter = seis_ref.shape[1] // XS
    halo = xs_ref.shape[2] - quarter

    def along_x(px):
        return {"tm": px * ZH + zh}

    def pieces(px):
        follow = (px + 1) % XS * quarter
        return [
            (seis_ref.at[:, pl.ds(pl.multiple_of(px * quarter, LANES), quarter)],
             xs_ref.at[x, :, 0:quarter]),
            (seis_ref.at[:, pl.ds(pl.multiple_of(follow, LANES), halo)],
             xs_ref.at[x, :, quarter : quarter + halo])]

    def send(kind, source, target, d, back):
        return pltpu.make_async_remote_copy(
            src_ref=source, dst_ref=target, send_sem=gs.at[kind, d], recv_sem=gr.at[kind, back],
            device_id=along_x((x + d) % XS), device_id_type=MESH)

    def tell(reach):
        for d in (reach, nz - reach):
            pl.semaphore_signal(ready.at[reach // 2], inc=1, device_id=place(y, (z + d) % nz, core),
                                device_id_type=MESH)

    def heard(reach):
        pl.semaphore_wait(ready.at[reach // 2], 2)

    def place(py, pz, pcore):
        return {"tm": x * ZH + pz // ZL, "tmpl": py * (ZL * CORES) + (pz % ZL) * CORES + pcore}

    other = place(y, z, 1 - core)
    ys = [(d - 1, (y + d) % YS) for d in (2, 1, 3)]
    zs = [(d - 1, (z + d) % nz) for d in sorted(range(1, nz), key=lambda d: abs(d - nz // 2))]
    barrier = pltpu.get_barrier_semaphore()
    targets = [place(y, (z + d) % nz, core) for d in (1, nz - 1)]
    targets += [place(py, z, core) for _, py in ys] + [other]
    targets += [along_x((x + d) % XS) for d in range(1, XS)]
    for target in targets:
        pl.semaphore_signal(barrier, inc=1, device_id=target, device_id_type=MESH)

    local = [pltpu.make_async_copy(wave_ref, tg_ref.at[x], gl.at[0]),
             pltpu.make_async_copy(shift_hbm, shift_ref, gl.at[3]),
             pltpu.make_async_copy(active_hbm, active_ref, gl.at[4])]
    local += [pltpu.make_async_copy(*pair, gl.at[1 + k]) for k, pair in enumerate(pieces(x))]
    for copy in local:
        copy.start()
    acc_ref[...] = jnp.zeros_like(acc_ref)
    nrows = xs_ref.shape[2] // LANES

    def multiply(s, c, part):
        frames = jnp.concatenate(
            [rows_ref[s, c, u + 16 * part : u + 16 * part + 16, :] for u in range(NF // BLK)], axis=1)
        for j in range(0, 16, 2):
            even = frames if j == 0 else pltpu.roll(frames, NF - SUB * j, 1)
            odd = pltpu.roll(frames, NF - SUB * (j + 1), 1)
            for k in range(2):
                top = k * LANES + SUB * j
                both = jnp.concatenate(
                    [even[SUB * k : SUB * k + SUB], odd[SUB * k : SUB * k + SUB]], axis=0)
                f_ref[top : top + 2 * SUB, :] = both.astype(jnp.bfloat16)
        acc_ref[part] += lax.dot_general(
            w_ref[s, c], f_ref[...], (((1,), (1,)), ((), ())), preferred_element_type=jnp.float32)

    def early(s):
        scale = active_ref[s * ZH + zh].astype(jnp.float32)
        column = lax.broadcasted_iota(jnp.int32, xs_ref.shape[1:], 1)
        last_quarter = jnp.full(xs_ref.shape[1:], x, jnp.int32) == XS - 1
        past = jnp.logical_and(last_quarter, column >= quarter)
        signal = jnp.where(past, 0.0, xs_ref[s].astype(jnp.float32) * scale)
        for c in range(CH):
            for r in range(nrows):
                rows_ref[s, c, r : r + 1, :] = signal[c : c + 1, r * LANES : (r + 1) * LANES]
        waves = [tg_ref[s, c].astype(jnp.float32) for c in range(CH)]
        for t in range(TPL):
            wave = jnp.concatenate([w[t : t + 1] for w in waves], axis=0)
            wide = jnp.concatenate([wave, jnp.zeros((CH, NF - L), jnp.float32)], axis=1)
            moved_ref[t, 0:CH, :] = pltpu.roll(wide, shift_ref[s * ZH + zh, t], 1)
        for c in range(CH):
            for at in range(0, TPL, 2):
                pair = []
                for slot in (at, at + 1):
                    t = (slot % 16) * 2 + slot // 16
                    wide = jnp.broadcast_to(moved_ref[t, c : c + 1, :], (SUB, NF))
                    pair.append(pltpu.roll(wide, 0, 1, stride=1, stride_axis=0))
                w_ref[s, c, at * SUB : (at + 2) * SUB, :] = jnp.concatenate(
                    pair, axis=0).astype(jnp.bfloat16)
            multiply(s, c, 0)

    def late(s):
        for c in range(CH):
            multiply(s, c, 1)

    away = pl.ds(pl.multiple_of((1 - core) * half, SUB), half)
    mine = pl.ds(pl.multiple_of(core * half, SUB), half)

    def to_core(part):
        return pltpu.make_async_remote_copy(
            src_ref=core_send.at[part], dst_ref=core_recv.at[part], send_sem=s1.at[part],
            recv_sem=r1.at[part], device_id=other, device_id_type=MESH)

    def to_y(part, d, py):
        return pltpu.make_async_remote_copy(
            src_ref=y_send.at[part, pl.ds(pl.multiple_of(py * block, block), block)],
            dst_ref=y_recv.at[part, d], send_sem=s2.at[part, d], recv_sem=r2.at[part, d],
            device_id=place(py, z, core), device_id_type=MESH)

    def after_core(part):
        to_core(part).wait()
        total = acc_ref[part, mine] + core_recv[part].astype(jnp.float32)
        sum_ref[part] = total
        y_send[part] = total.astype(jnp.bfloat16)
        for d, py in ys:
            to_y(part, d, py).start()

    gather = []
    for c in range(CH):
        for d in (3, 1):
            gather.append(send(c, wave_ref.at[c], tg_ref.at[x, c], d, XS - d))
    for d in (3, 1, 2):
        for k, (source, target) in enumerate(pieces((x + d) % XS)):
            gather.append(send(CH + k, source, target, d, XS - d))
    relay = []
    for c in range(CH):
        onward = tg_ref.at[(x + 1) % XS, c]
        relay.append(pltpu.make_async_remote_copy(
            src_ref=onward, dst_ref=onward, send_sem=gs.at[c, 2], recv_sem=gr.at[c, 2],
            device_id=along_x((x + 3) % XS), device_id_type=MESH))
    pl.semaphore_wait(barrier, len(targets))
    for copy in gather:
        copy.start()
    tell(1)
    for copy in local:
        copy.wait()

    def arrive(step, carry):
        offset = step ^ (step // 2)
        s = (x + offset) % XS

        @pl.when(step > 0)
        def _():
            for c in range(CH):
                send(c, wave_ref.at[c], tg_ref.at[s, c], 1, offset).wait_recv()

                @pl.when(step == 1)
                def _():
                    relay[c].start()

            for k, (source, _) in enumerate(pieces(x)):
                target = xs_ref.at[s, :, k * quarter : k * quarter + source.shape[1]]
                send(CH + k, source, target, 1, offset).wait_recv()

        @pl.when(step == 1)
        def _():
            heard(1)
            tell(2)

        @pl.when(step == 2)
        def _():
            heard(2)
            tell(4)

        early(s)

        @pl.when(step < XS - 1)
        def _():
            late(s)

        return carry

    lax.fori_loop(0, XS, arrive, 0)
    core_send[0] = acc_ref[0, away].astype(jnp.bfloat16)
    to_core(0).start()
    late((x + 2) % XS)
    core_send[1] = acc_ref[1, away].astype(jnp.bfloat16)
    to_core(1).start()
    after_core(0)
    after_core(1)
    for copy in gather + relay:
        copy.wait_send()

    last = [
        pltpu.make_async_remote_copy(
            src_ref=z_send.at[pz], dst_ref=z_recv.at[d], send_sem=s3.at[d], recv_sem=r3.at[d],
            device_id=place(y, pz, core), device_id_type=MESH)
        for d, pz in zs]
    heard(4)
    for part in range(2):
        total = sum_ref[part, pl.ds(pl.multiple_of(y * block, block), block)]
        for d, py in ys:
            to_y(part, d, py).wait()
            total = total + y_recv[part, d].astype(jnp.float32)
        for pzl in range(ZL):
            for k in range(2):
                tile = total[pzl * SUB : (pzl + 1) * SUB, k * LANES : (k + 1) * LANES]
                at = (2 * part + k) * ZL + pzl
                plane_ref[at] = tile
                z_send[at] = tile.astype(jnp.bfloat16)
        for copy, (_, pz) in zip(last, zs):
            pl.when(pz // (nz // 2) == part)(copy.start)

    for copy in last:
        copy.wait()
    total = plane_ref[z]
    for d in range(nz - 1):
        total = total + z_recv[d].astype(jnp.float32)
    out_ref[...] = transpose_groups(total)


def per_device(seismic, templates, moveout, active):
    window = seismic.shape[2]
    span = window // XS + NF
    dma = pltpu.SemaphoreType.DMA
    rows, columns = TPL * SUB, window // XS // SUB // 2
    half = rows // CORES
    block = half // YS
    devices = ZL * ZH
    bf16, f32 = jnp.bfloat16, jnp.float32
    tile = pl.pallas_call(
        stack_kernel,
        out_shape=jax.ShapeDtypeStruct((SUB, LANES), f32),
        in_specs=[pl.BlockSpec(memory_space=pl.ANY)] * 4,
        out_specs=pl.BlockSpec(memory_space=pltpu.VMEM),
        scratch_shapes=[pltpu.SMEM(moveout.shape, moveout.dtype),
                        pltpu.SMEM(active.shape, active.dtype),
                        pltpu.VMEM((XS, CH, span), bf16),
                        pltpu.VMEM((XS, CH, TPL, L), bf16),
                        dma((CH + 2, XS)), dma((CH + 2, XS)), dma((5,)),
                        pltpu.VMEM((XS, CH, 40, LANES), f32),
                        pltpu.VMEM((TPL, SUB, NF), f32),
                        pltpu.VMEM((XS, CH, rows, NF), bf16),
                        pltpu.VMEM((columns, NF), bf16),
                        pltpu.VMEM((2, rows, columns), f32),
                        pltpu.VMEM((2, half, columns), bf16),
                        pltpu.VMEM((2, half, columns), bf16),
                        pltpu.VMEM((2, half, columns), f32),
                        pltpu.VMEM((2, half, columns), bf16),
                        pltpu.VMEM((2, YS - 1, block, columns), bf16),
                        pltpu.VMEM((devices, SUB, LANES), f32),
                        pltpu.VMEM((devices, SUB, LANES), bf16),
                        pltpu.VMEM((devices - 1, SUB, LANES), bf16),
                        dma((2,)), dma((2,)), dma((2, YS - 1)), dma((2, YS - 1)),
                        dma((devices - 1,)), dma((devices - 1,)),
                        pltpu.SemaphoreType.REGULAR((3,))],
        compiler_params=pltpu.CompilerParams(collective_id=0, has_side_effects=True),
        name="stack",
    )(moveout, active, seismic[0], templates[0].transpose(1, 0, 2))
    return tile.reshape(1, SUB * LANES)


def solution(mesh):
    in_specs = (
        P(("tmpl", "tm"), None, None),
        P(("tmpl", "tm"), None, None, None),
        P("tmpl", None),
        P("tmpl"),
    )
    out_specs = P("tmpl", "tm")
    return jax.shard_map(
        per_device, mesh=mesh, in_specs=in_specs, out_specs=out_specs, check_vma=False
    )
```

```python
import jax
import jax.numpy as jnp
from jax import lax
from jax.experimental import pallas as pl
from jax.experimental.pallas import tpu as pltpu
from jax.sharding import PartitionSpec as P

XS, ZH = 4, 4
YS, ZL, CORES = 4, 4, 2
CH = 3
L = 256
NF = 512
BLK = 128
TPL = 32
LANES = 128
SUB = 8
MESH = pl.DeviceIdType.MESH


def transpose_groups(tile):
    row = lax.broadcasted_iota(jnp.int32, tile.shape, 0)
    lane = lax.broadcasted_iota(jnp.int32, tile.shape, 1)
    for bit in (1, 2, 4):
        below = pltpu.roll(pltpu.roll(tile, SUB - bit, 0), bit, 1)
        above = pltpu.roll(pltpu.roll(tile, bit, 0), LANES - bit, 1)
        low, left = (row & bit) == 0, (lane & bit) == 0
        tile = jnp.where(low == left, tile, jnp.where(low, below, above))
    return tile


def stack_kernel(shift_hbm, active_hbm, seis_ref, wave_ref, out_ref,
                 shift_ref, active_ref, xs_ref, tg_ref, gs, gr, gl, rows_ref, moved_ref, w_ref, f_ref, acc_ref,
                 core_send, core_recv, sum_ref, y_send, y_recv, plane_ref, z_send, z_recv,
                 s1, r1, s2, r2, s3, r3, ready):
    tm, tmpl = lax.axis_index("tm"), lax.axis_index("tmpl")
    x, zh = tm // ZH, tm % ZH
    y, zl, core = tmpl // (ZL * CORES), (tmpl // CORES) % ZL, tmpl % CORES
    nz = ZL * ZH
    z = zh * ZL + zl
    half = acc_ref.shape[1] // CORES
    block = half // YS

    quarter = seis_ref.shape[1] // XS
    halo = xs_ref.shape[2] - quarter

    def along_x(px):
        return {"tm": px * ZH + zh}

    def pieces(px):
        follow = (px + 1) % XS * quarter
        return [
            (seis_ref.at[:, pl.ds(pl.multiple_of(px * quarter, LANES), quarter)],
             xs_ref.at[x, :, 0:quarter]),
            (seis_ref.at[:, pl.ds(pl.multiple_of(follow, LANES), halo)],
             xs_ref.at[x, :, quarter : quarter + halo])]

    def send(kind, source, target, d, back):
        return pltpu.make_async_remote_copy(
            src_ref=source, dst_ref=target, send_sem=gs.at[kind, d], recv_sem=gr.at[kind, back],
            device_id=along_x((x + d) % XS), device_id_type=MESH)

    def tell(reach):
        for d in (reach, nz - reach):
            pl.semaphore_signal(ready.at[reach // 2], inc=1, device_id=place(y, (z + d) % nz, core),
                                device_id_type=MESH)

    def heard(reach):
        pl.semaphore_wait(ready.at[reach // 2], 2)

    def place(py, pz, pcore):
        return {"tm": x * ZH + pz // ZL, "tmpl": py * (ZL * CORES) + (pz % ZL) * CORES + pcore}

    other = place(y, z, 1 - core)
    ys = [(d - 1, (y + d) % YS) for d in (2, 1, 3)]
    zs = [(d - 1, (z + d) % nz) for d in sorted(range(1, nz), key=lambda d: abs(d - nz // 2))]
    barrier = pltpu.get_barrier_semaphore()
    targets = [place(y, (z + d) % nz, core) for d in (1, nz - 1)]
    targets += [place(py, z, core) for _, py in ys] + [other]
    targets += [along_x((x + d) % XS) for d in range(1, XS)]
    for target in targets:
        pl.semaphore_signal(barrier, inc=1, device_id=target, device_id_type=MESH)

    local = [pltpu.make_async_copy(wave_ref, tg_ref.at[x], gl.at[0]),
             pltpu.make_async_copy(shift_hbm, shift_ref, gl.at[3]),
             pltpu.make_async_copy(active_hbm, active_ref, gl.at[4])]
    local += [pltpu.make_async_copy(*pair, gl.at[1 + k]) for k, pair in enumerate(pieces(x))]
    for copy in local:
        copy.start()
    acc_ref[...] = jnp.zeros_like(acc_ref)
    nrows = xs_ref.shape[2] // LANES

    def sample_frames(s):
        scale = active_ref[s * ZH + zh].astype(jnp.float32)
        column = lax.broadcasted_iota(jnp.int32, xs_ref.shape[1:], 1)
        last_quarter = jnp.full(xs_ref.shape[1:], x, jnp.int32) == XS - 1
        past = jnp.logical_and(last_quarter, column >= quarter)
        signal = jnp.where(past, 0.0, xs_ref[s].astype(jnp.float32) * scale)
        for c in range(CH):
            for r in range(nrows):
                rows_ref[c, r : r + 1, :] = signal[c : c + 1, r * LANES : (r + 1) * LANES]
        for c in range(CH):
            frames = jnp.concatenate([rows_ref[c, u : u + 32, :] for u in range(NF // BLK)], axis=1)
            for j in range(0, 16, 2):
                even = frames if j == 0 else pltpu.roll(frames, NF - SUB * j, 1)
                odd = pltpu.roll(frames, NF - SUB * (j + 1), 1)
                for k in range(ZH):
                    top = k % 2 * LANES + SUB * j
                    both = jnp.concatenate(
                        [even[SUB * k : SUB * k + SUB], odd[SUB * k : SUB * k + SUB]], axis=0)
                    f_ref[c, k // 2, top : top + 2 * SUB, :] = both.astype(jnp.bfloat16)

    def template_rows(s):
        waves = [tg_ref[s, c].astype(jnp.float32) for c in range(CH)]
        for t in range(TPL):
            wave = jnp.concatenate([w[t : t + 1] for w in waves], axis=0)
            wide = jnp.concatenate([wave, jnp.zeros((CH, NF - L), jnp.float32)], axis=1)
            moved_ref[t, 0:CH, :] = pltpu.roll(wide, shift_ref[s * ZH + zh, t], 1)
        for c in range(CH):
            for at in range(0, TPL, 2):
                pair = []
                for slot in (at, at + 1):
                    t = (slot % 16) * 2 + slot // 16
                    wide = jnp.broadcast_to(moved_ref[t, c : c + 1, :], (SUB, NF))
                    pair.append(pltpu.roll(wide, 0, 1, stride=1, stride_axis=0))
                w_ref[c, at * SUB : (at + 2) * SUB, :] = jnp.concatenate(
                    pair, axis=0).astype(jnp.bfloat16)

    def multiply(part):
        for c in range(CH):
            acc_ref[part] += lax.dot_general(
                w_ref[c], f_ref[c, part], (((1,), (1,)), ((), ())),
                preferred_element_type=jnp.float32)

    away = pl.ds(pl.multiple_of((1 - core) * half, SUB), half)
    mine = pl.ds(pl.multiple_of(core * half, SUB), half)

    def to_core(part):
        return pltpu.make_async_remote_copy(
            src_ref=core_send.at[part], dst_ref=core_recv.at[part], send_sem=s1.at[part],
            recv_sem=r1.at[part], device_id=other, device_id_type=MESH)

    def to_y(part, d, py):
        return pltpu.make_async_remote_copy(
            src_ref=y_send.at[part, pl.ds(pl.multiple_of(py * block, block), block)],
            dst_ref=y_recv.at[part, d], send_sem=s2.at[part, d], recv_sem=r2.at[part, d],
            device_id=place(py, z, core), device_id_type=MESH)

    def after_core(part):
        to_core(part).wait()
        total = acc_ref[part, mine] + core_recv[part].astype(jnp.float32)
        sum_ref[part] = total
        y_send[part] = total.astype(jnp.bfloat16)
        for d, py in ys:
            to_y(part, d, py).start()

    gather = []
    for c in range(CH):
        for d in (3, 1):
            gather.append(send(c, wave_ref.at[c], tg_ref.at[x, c], d, XS - d))
    for d in (3, 1, 2):
        for k, (source, target) in enumerate(pieces((x + d) % XS)):
            gather.append(send(CH + k, source, target, d, XS - d))
    relay = []
    for c in range(CH):
        onward = tg_ref.at[(x + 1) % XS, c]
        relay.append(pltpu.make_async_remote_copy(
            src_ref=onward, dst_ref=onward, send_sem=gs.at[c, 2], recv_sem=gr.at[c, 2],
            device_id=along_x((x + 3) % XS), device_id_type=MESH))
    pl.semaphore_wait(barrier, len(targets))
    for copy in gather:
        copy.start()
    tell(1)
    for copy in local:
        copy.wait()

    def arrive(step, carry):
        offset = step ^ (step // 2)
        s = (x + offset) % XS

        def templates_here(c):
            send(c, wave_ref.at[c], tg_ref.at[s, c], 1, offset).wait_recv()

        @pl.when(step == 1)
        def _():
            for c in range(CH):
                templates_here(c)
                relay[c].start()

        @pl.when(step > 0)
        def _():
            for k, (source, _) in enumerate(pieces(x)):
                target = xs_ref.at[s, :, k * quarter : k * quarter + source.shape[1]]
                send(CH + k, source, target, 1, offset).wait_recv()

        @pl.when(step == 1)
        def _():
            heard(1)
            tell(2)

        @pl.when(step == 2)
        def _():
            heard(2)
            tell(4)

        sample_frames(s)

        @pl.when(step > 1)
        def _():
            for c in range(CH):
                templates_here(c)

        template_rows(s)
        multiply(0)

        @pl.when(step < XS - 1)
        def _():
            multiply(1)

        return carry

    lax.fori_loop(0, XS, arrive, 0)
    core_send[0] = acc_ref[0, away].astype(jnp.bfloat16)
    to_core(0).start()
    multiply(1)
    core_send[1] = acc_ref[1, away].astype(jnp.bfloat16)
    to_core(1).start()
    after_core(0)
    after_core(1)
    for copy in gather + relay:
        copy.wait_send()

    last = [
        pltpu.make_async_remote_copy(
            src_ref=z_send.at[pz], dst_ref=z_recv.at[d], send_sem=s3.at[d], recv_sem=r3.at[d],
            device_id=place(y, pz, core), device_id_type=MESH)
        for d, pz in zs]
    heard(4)
    for part in range(2):
        total = sum_ref[part, pl.ds(pl.multiple_of(y * block, block), block)]
        for d, py in ys:
            to_y(part, d, py).wait()
            total = total + y_recv[part, d].astype(jnp.float32)
        for pzl in range(ZL):
            for k in range(2):
                tile = total[pzl * SUB : (pzl + 1) * SUB, k * LANES : (k + 1) * LANES]
                at = (2 * part + k) * ZL + pzl
                plane_ref[at] = tile
                z_send[at] = tile.astype(jnp.bfloat16)
        for copy, (_, pz) in zip(last, zs):
            pl.when(pz // (nz // 2) == part)(copy.start)

    for copy in last:
        copy.wait()
    total = plane_ref[z]
    for d in range(nz - 1):
        total = total + z_recv[d].astype(jnp.float32)
    out_ref[...] = transpose_groups(total)


def per_device(seismic, templates, moveout, active):
    window = seismic.shape[2]
    span = window // XS + NF
    dma = pltpu.SemaphoreType.DMA
    rows, columns = TPL * SUB, window // XS // SUB // 2
    half = rows // CORES
    block = half // YS
    devices = ZL * ZH
    bf16, f32 = jnp.bfloat16, jnp.float32
    tile = pl.pallas_call(
        stack_kernel,
        out_shape=jax.ShapeDtypeStruct((SUB, LANES), f32),
        in_specs=[pl.BlockSpec(memory_space=pl.ANY)] * 4,
        out_specs=pl.BlockSpec(memory_space=pltpu.VMEM),
        scratch_shapes=[pltpu.SMEM(moveout.shape, moveout.dtype),
                        pltpu.SMEM(active.shape, active.dtype),
                        pltpu.VMEM((XS, CH, span), bf16),
                        pltpu.VMEM((XS, CH, TPL, L), bf16),
                        dma((CH + 2, XS)), dma((CH + 2, XS)), dma((5,)),
                        pltpu.VMEM((CH, 40, LANES), f32),
                        pltpu.VMEM((TPL, SUB, NF), f32),
                        pltpu.VMEM((CH, rows, NF), bf16),
                        pltpu.VMEM((CH, 2, columns, NF), bf16),
                        pltpu.VMEM((2, rows, columns), f32),
                        pltpu.VMEM((2, half, columns), bf16),
                        pltpu.VMEM((2, half, columns), bf16),
                        pltpu.VMEM((2, half, columns), f32),
                        pltpu.VMEM((2, half, columns), bf16),
                        pltpu.VMEM((2, YS - 1, block, columns), bf16),
                        pltpu.VMEM((devices, SUB, LANES), f32),
                        pltpu.VMEM((devices, SUB, LANES), bf16),
                        pltpu.VMEM((devices - 1, SUB, LANES), bf16),
                        dma((2,)), dma((2,)), dma((2, YS - 1)), dma((2, YS - 1)),
                        dma((devices - 1,)), dma((devices - 1,)),
                        pltpu.SemaphoreType.REGULAR((3,))],
        compiler_params=pltpu.CompilerParams(collective_id=0, has_side_effects=True),
        name="stack",
    )(moveout, active, seismic[0], templates[0].transpose(1, 0, 2))
    return tile.reshape(1, SUB * LANES)


def solution(mesh):
    in_specs = (
        P(("tmpl", "tm"), None, None),
        P(("tmpl", "tm"), None, None, None),
        P("tmpl", None),
        P("tmpl"),
    )
    out_specs = P("tmpl", "tm")
    return jax.shard_map(
        per_device, mesh=mesh, in_specs=in_specs, out_specs=out_specs, check_vma=False
    )
```

```python
import jax
import jax.numpy as jnp
from jax import lax
from jax.experimental import pallas as pl
from jax.experimental.pallas import tpu as pltpu
from jax.sharding import PartitionSpec as P

XS, ZH = 4, 4
YS, ZL, CORES = 4, 4, 2
CH = 3
L = 256
NF = 512
BLK = 128
TPL = 32
LANES = 128
SUB = 8
MESH = pl.DeviceIdType.MESH


def transpose_groups(tile):
    row = lax.broadcasted_iota(jnp.int32, tile.shape, 0)
    lane = lax.broadcasted_iota(jnp.int32, tile.shape, 1)
    for bit in (1, 2, 4):
        below = pltpu.roll(pltpu.roll(tile, SUB - bit, 0), bit, 1)
        above = pltpu.roll(pltpu.roll(tile, bit, 0), LANES - bit, 1)
        low, left = (row & bit) == 0, (lane & bit) == 0
        tile = jnp.where(low == left, tile, jnp.where(low, below, above))
    return tile


def stack_kernel(shift_hbm, active_hbm, seis_ref, wave_ref, out_ref,
                 shift_ref, active_ref, xs_ref, tg_ref, gs, gr, gl, rows_ref, moved_ref, w_ref, f_ref, acc_ref,
                 core_send, core_recv, sum_ref, y_send, y_recv, plane_ref, z_send, z_recv,
                 s1, r1, s2, r2, s3, r3, ready):
    tm, tmpl = lax.axis_index("tm"), lax.axis_index("tmpl")
    x, zh = tm // ZH, tm % ZH
    y, zl, core = tmpl // (ZL * CORES), (tmpl // CORES) % ZL, tmpl % CORES
    nz = ZL * ZH
    z = zh * ZL + zl
    half = acc_ref.shape[1] // CORES
    block = half // YS

    quarter = seis_ref.shape[1] // XS
    halo = xs_ref.shape[2] - quarter

    def along_x(px):
        return {"tm": px * ZH + zh}

    def pieces(px):
        follow = (px + 1) % XS * quarter
        return [
            (seis_ref.at[:, pl.ds(pl.multiple_of(px * quarter, LANES), quarter)],
             xs_ref.at[x, :, 0:quarter]),
            (seis_ref.at[:, pl.ds(pl.multiple_of(follow, LANES), halo)],
             xs_ref.at[x, :, quarter : quarter + halo])]

    def send(kind, source, target, d, back):
        return pltpu.make_async_remote_copy(
            src_ref=source, dst_ref=target, send_sem=gs.at[kind, d], recv_sem=gr.at[kind, back],
            device_id=along_x((x + d) % XS), device_id_type=MESH)

    def tell(reach):
        for d in (reach, nz - reach):
            pl.semaphore_signal(ready.at[reach // 2], inc=1, device_id=place(y, (z + d) % nz, core),
                                device_id_type=MESH)

    def heard(reach):
        pl.semaphore_wait(ready.at[reach // 2], 2)

    def place(py, pz, pcore):
        return {"tm": x * ZH + pz // ZL, "tmpl": py * (ZL * CORES) + (pz % ZL) * CORES + pcore}

    other = place(y, z, 1 - core)
    ys = [(d - 1, (y + d) % YS) for d in (2, 1, 3)]
    zs = [(d - 1, (z + d) % nz) for d in sorted(range(1, nz), key=lambda d: abs(d - nz // 2))]
    barrier = pltpu.get_barrier_semaphore()
    targets = [place(y, (z + d) % nz, core) for d in (1, nz - 1)]
    targets += [place(py, z, core) for _, py in ys] + [other]
    targets += [along_x((x + d) % XS) for d in range(1, XS)]
    for target in targets:
        pl.semaphore_signal(barrier, inc=1, device_id=target, device_id_type=MESH)

    local = [pltpu.make_async_copy(wave_ref, tg_ref.at[x], gl.at[0]),
             pltpu.make_async_copy(shift_hbm, shift_ref, gl.at[3]),
             pltpu.make_async_copy(active_hbm, active_ref, gl.at[4])]
    local += [pltpu.make_async_copy(*pair, gl.at[1 + k]) for k, pair in enumerate(pieces(x))]
    for copy in local:
        copy.start()
    acc_ref[...] = jnp.zeros_like(acc_ref)
    nrows = xs_ref.shape[2] // LANES

    def multiply(s, c, part):
        frames = jnp.concatenate(
            [rows_ref[s, c, u + 16 * part : u + 16 * part + 16, :] for u in range(NF // BLK)], axis=1)
        for j in range(0, 16, 2):
            even = frames if j == 0 else pltpu.roll(frames, NF - SUB * j, 1)
            odd = pltpu.roll(frames, NF - SUB * (j + 1), 1)
            for k in range(2):
                top = k * LANES + SUB * j
                both = jnp.concatenate(
                    [even[SUB * k : SUB * k + SUB], odd[SUB * k : SUB * k + SUB]], axis=0)
                f_ref[top : top + 2 * SUB, :] = both.astype(jnp.bfloat16)
        acc_ref[part] += lax.dot_general(
            w_ref[s, c], f_ref[...], (((1,), (1,)), ((), ())), preferred_element_type=jnp.float32)

    def early(s):
        scale = active_ref[s * ZH + zh].astype(jnp.float32)
        column = lax.broadcasted_iota(jnp.int32, xs_ref.shape[1:], 1)
        last_quarter = jnp.full(xs_ref.shape[1:], x, jnp.int32) == XS - 1
        past = jnp.logical_and(last_quarter, column >= quarter)
        signal = jnp.where(past, 0.0, xs_ref[s].astype(jnp.float32) * scale)
        for c in range(CH):
            for r in range(nrows):
                rows_ref[s, c, r : r + 1, :] = signal[c : c + 1, r * LANES : (r + 1) * LANES]
        waves = [tg_ref[s, c].astype(jnp.float32) for c in range(CH)]
        for t in range(TPL):
            wave = jnp.concatenate([w[t : t + 1] for w in waves], axis=0)
            wide = jnp.concatenate([wave, jnp.zeros((CH, NF - L), jnp.float32)], axis=1)
            moved_ref[t, 0:CH, :] = pltpu.roll(wide, shift_ref[s * ZH + zh, t], 1)
        for c in range(CH):
            for at in range(0, TPL, 2):
                pair = []
                for slot in (at, at + 1):
                    t = (slot % 16) * 2 + slot // 16
                    wide = jnp.broadcast_to(moved_ref[t, c : c + 1, :], (SUB, NF))
                    pair.append(pltpu.roll(wide, 0, 1, stride=1, stride_axis=0))
                w_ref[s, c, at * SUB : (at + 2) * SUB, :] = jnp.concatenate(
                    pair, axis=0).astype(jnp.bfloat16)
            multiply(s, c, 0)

    def late(s):
        for c in range(CH):
            multiply(s, c, 1)

    away = pl.ds(pl.multiple_of((1 - core) * half, SUB), half)
    mine = pl.ds(pl.multiple_of(core * half, SUB), half)

    def to_core(part):
        return pltpu.make_async_remote_copy(
            src_ref=core_send.at[part], dst_ref=core_recv.at[part], send_sem=s1.at[part],
            recv_sem=r1.at[part], device_id=other, device_id_type=MESH)

    def to_y(part, d, py):
        return pltpu.make_async_remote_copy(
            src_ref=y_send.at[part, pl.ds(pl.multiple_of(py * block, block), block)],
            dst_ref=y_recv.at[part, d], send_sem=s2.at[part, d], recv_sem=r2.at[part, d],
            device_id=place(py, z, core), device_id_type=MESH)

    def after_core(part):
        to_core(part).wait()
        total = acc_ref[part, mine] + core_recv[part].astype(jnp.float32)
        sum_ref[part] = total
        y_send[part] = total.astype(jnp.bfloat16)
        for d, py in ys:
            to_y(part, d, py).start()

    gather = []
    def samples(d):
        for k, (source, target) in enumerate(pieces((x + d) % XS)):
            gather.append(send(CH + k, source, target, d, XS - d))

    def waveforms(d):
        for c in range(CH):
            gather.append(send(c, wave_ref.at[c], tg_ref.at[x, c], d, XS - d))

    waveforms(3)
    samples(2)
    waveforms(1)
    samples(3)
    samples(1)
    relay = []
    for c in range(CH):
        onward = tg_ref.at[(x + 1) % XS, c]
        relay.append(pltpu.make_async_remote_copy(
            src_ref=onward, dst_ref=onward, send_sem=gs.at[c, 2], recv_sem=gr.at[c, 2],
            device_id=along_x((x + 3) % XS), device_id_type=MESH))
    pl.semaphore_wait(barrier, len(targets))
    for copy in gather:
        copy.start()
    tell(1)
    for copy in local:
        copy.wait()

    def arrive(step, carry):
        offset = step ^ (step // 2)
        s = (x + offset) % XS

        @pl.when(step > 0)
        def _():
            for c in range(CH):
                send(c, wave_ref.at[c], tg_ref.at[s, c], 1, offset).wait_recv()

                @pl.when(step == 1)
                def _():
                    relay[c].start()

            for k, (source, _) in enumerate(pieces(x)):
                target = xs_ref.at[s, :, k * quarter : k * quarter + source.shape[1]]
                send(CH + k, source, target, 1, offset).wait_recv()

        @pl.when(step == 1)
        def _():
            heard(1)
            tell(2)

        @pl.when(step == 2)
        def _():
            heard(2)
            tell(4)

        early(s)

        @pl.when(step < XS - 1)
        def _():
            late(s)

        return carry

    lax.fori_loop(0, XS, arrive, 0)
    core_send[0] = acc_ref[0, away].astype(jnp.bfloat16)
    to_core(0).start()
    late((x + 2) % XS)
    core_send[1] = acc_ref[1, away].astype(jnp.bfloat16)
    to_core(1).start()
    after_core(0)
    after_core(1)
    for copy in gather + relay:
        copy.wait_send()

    last = [
        pltpu.make_async_remote_copy(
            src_ref=z_send.at[pz], dst_ref=z_recv.at[d], send_sem=s3.at[d], recv_sem=r3.at[d],
            device_id=place(y, pz, core), device_id_type=MESH)
        for d, pz in zs]
    heard(4)
    for part in range(2):
        total = sum_ref[part, pl.ds(pl.multiple_of(y * block, block), block)]
        for d, py in ys:
            to_y(part, d, py).wait()
            total = total + y_recv[part, d].astype(jnp.float32)
        for pzl in range(ZL):
            for k in range(2):
                tile = total[pzl * SUB : (pzl + 1) * SUB, k * LANES : (k + 1) * LANES]
                at = (2 * part + k) * ZL + pzl
                plane_ref[at] = tile
                z_send[at] = tile.astype(jnp.bfloat16)
        for copy, (_, pz) in zip(last, zs):
            pl.when(pz // (nz // 2) == part)(copy.start)

    for copy in last:
        copy.wait()
    total = plane_ref[z]
    for d in range(nz - 1):
        total = total + z_recv[d].astype(jnp.float32)
    out_ref[...] = transpose_groups(total)


def per_device(seismic, templates, moveout, active):
    window = seismic.shape[2]
    span = window // XS + NF
    dma = pltpu.SemaphoreType.DMA
    rows, columns = TPL * SUB, window // XS // SUB // 2
    half = rows // CORES
    block = half // YS
    devices = ZL * ZH
    bf16, f32 = jnp.bfloat16, jnp.float32
    tile = pl.pallas_call(
        stack_kernel,
        out_shape=jax.ShapeDtypeStruct((SUB, LANES), f32),
        in_specs=[pl.BlockSpec(memory_space=pl.ANY)] * 4,
        out_specs=pl.BlockSpec(memory_space=pltpu.VMEM),
        scratch_shapes=[pltpu.SMEM(moveout.shape, moveout.dtype),
                        pltpu.SMEM(active.shape, active.dtype),
                        pltpu.VMEM((XS, CH, span), bf16),
                        pltpu.VMEM((XS, CH, TPL, L), bf16),
                        dma((CH + 2, XS)), dma((CH + 2, XS)), dma((5,)),
                        pltpu.VMEM((XS, CH, 40, LANES), f32),
                        pltpu.VMEM((TPL, SUB, NF), f32),
                        pltpu.VMEM((XS, CH, rows, NF), bf16),
                        pltpu.VMEM((columns, NF), bf16),
                        pltpu.VMEM((2, rows, columns), f32),
                        pltpu.VMEM((2, half, columns), bf16),
                        pltpu.VMEM((2, half, columns), bf16),
                        pltpu.VMEM((2, half, columns), f32),
                        pltpu.VMEM((2, half, columns), bf16),
                        pltpu.VMEM((2, YS - 1, block, columns), bf16),
                        pltpu.VMEM((devices, SUB, LANES), f32),
                        pltpu.VMEM((devices, SUB, LANES), bf16),
                        pltpu.VMEM((devices - 1, SUB, LANES), bf16),
                        dma((2,)), dma((2,)), dma((2, YS - 1)), dma((2, YS - 1)),
                        dma((devices - 1,)), dma((devices - 1,)),
                        pltpu.SemaphoreType.REGULAR((3,))],
        compiler_params=pltpu.CompilerParams(collective_id=0, has_side_effects=True),
        name="stack",
    )(moveout, active, seismic[0], templates[0].transpose(1, 0, 2))
    return tile.reshape(1, SUB * LANES)


def solution(mesh):
    in_specs = (
        P(("tmpl", "tm"), None, None),
        P(("tmpl", "tm"), None, None, None),
        P("tmpl", None),
        P("tmpl"),
    )
    out_specs = P("tmpl", "tm")
    return jax.shard_map(
        per_device, mesh=mesh, in_specs=in_specs, out_specs=out_specs, check_vma=False
    )
```

```python
import jax
import jax.numpy as jnp
from jax import lax
from jax.experimental import pallas as pl
from jax.experimental.pallas import tpu as pltpu
from jax.sharding import PartitionSpec as P

XS, ZH = 4, 4
YS, ZL, CORES = 4, 4, 2
CH = 3
L = 256
NF = 512
BLK = 128
TPL = 32
LANES = 128
SUB = 8
MESH = pl.DeviceIdType.MESH


def transpose_groups(tile):
    row = lax.broadcasted_iota(jnp.int32, tile.shape, 0)
    lane = lax.broadcasted_iota(jnp.int32, tile.shape, 1)
    for bit in (1, 2, 4):
        below = pltpu.roll(pltpu.roll(tile, SUB - bit, 0), bit, 1)
        above = pltpu.roll(pltpu.roll(tile, bit, 0), LANES - bit, 1)
        low, left = (row & bit) == 0, (lane & bit) == 0
        tile = jnp.where(low == left, tile, jnp.where(low, below, above))
    return tile


def stack_kernel(shift_hbm, active_hbm, seis_ref, wave_ref, out_ref,
                 shift_ref, active_ref, xs_ref, tg_ref, gs, gr, gl, rows_ref, moved_ref, w_ref, f_ref, acc_ref,
                 core_send, core_recv, sum_ref, y_send, y_recv, plane_ref, z_send, z_recv,
                 s1, r1, s2, r2, s3, r3, ready):
    tm, tmpl = lax.axis_index("tm"), lax.axis_index("tmpl")
    x, zh = tm // ZH, tm % ZH
    y, zl, core = tmpl // (ZL * CORES), (tmpl // CORES) % ZL, tmpl % CORES
    nz = ZL * ZH
    z = zh * ZL + zl
    half = acc_ref.shape[1] // CORES
    block = half // YS

    quarter = seis_ref.shape[1] // XS
    halo = xs_ref.shape[2] - quarter

    def along_x(px):
        return {"tm": px * ZH + zh}

    def pieces(px):
        follow = (px + 1) % XS * quarter
        return [
            (seis_ref.at[:, pl.ds(pl.multiple_of(px * quarter, LANES), quarter)],
             xs_ref.at[x, :, 0:quarter]),
            (seis_ref.at[:, pl.ds(pl.multiple_of(follow, LANES), halo)],
             xs_ref.at[x, :, quarter : quarter + halo])]

    def send(kind, source, target, d, back):
        return pltpu.make_async_remote_copy(
            src_ref=source, dst_ref=target, send_sem=gs.at[kind, d], recv_sem=gr.at[kind, back],
            device_id=along_x((x + d) % XS), device_id_type=MESH)

    def tell(reach):
        for d in (reach, nz - reach):
            pl.semaphore_signal(ready.at[reach // 2], inc=1, device_id=place(y, (z + d) % nz, core),
                                device_id_type=MESH)

    def heard(reach):
        pl.semaphore_wait(ready.at[reach // 2], 2)

    def place(py, pz, pcore):
        return {"tm": x * ZH + pz // ZL, "tmpl": py * (ZL * CORES) + (pz % ZL) * CORES + pcore}

    other = place(y, z, 1 - core)
    ys = [(d - 1, (y + d) % YS) for d in (2, 1, 3)]
    zs = [(d - 1, (z + d) % nz) for d in sorted(range(1, nz), key=lambda d: abs(d - nz // 2))]
    barrier = pltpu.get_barrier_semaphore()
    targets = [place(y, (z + d) % nz, core) for d in (1, nz - 1)]
    targets += [place(py, z, core) for _, py in ys] + [other]
    targets += [along_x((x + d) % XS) for d in range(1, XS)]
    for target in targets:
        pl.semaphore_signal(barrier, inc=1, device_id=target, device_id_type=MESH)

    local = [pltpu.make_async_copy(wave_ref, tg_ref.at[x], gl.at[0]),
             pltpu.make_async_copy(shift_hbm, shift_ref, gl.at[3]),
             pltpu.make_async_copy(active_hbm, active_ref, gl.at[4])]
    local += [pltpu.make_async_copy(*pair, gl.at[1 + k]) for k, pair in enumerate(pieces(x))]
    for copy in local:
        copy.start()
    acc_ref[...] = jnp.zeros_like(acc_ref)
    nrows = xs_ref.shape[2] // LANES

    def multiply(s, c, part):
        frames = jnp.concatenate(
            [rows_ref[s, c, u + 16 * part : u + 16 * part + 16, :] for u in range(NF // BLK)], axis=1)
        for j in range(0, 16, 2):
            even = frames if j == 0 else pltpu.roll(frames, NF - SUB * j, 1)
            odd = pltpu.roll(frames, NF - SUB * (j + 1), 1)
            for k in range(2):
                top = k * LANES + SUB * j
                both = jnp.concatenate(
                    [even[SUB * k : SUB * k + SUB], odd[SUB * k : SUB * k + SUB]], axis=0)
                f_ref[top : top + 2 * SUB, :] = both.astype(jnp.bfloat16)
        acc_ref[part] += lax.dot_general(
            w_ref[s, c], f_ref[...], (((1,), (1,)), ((), ())), preferred_element_type=jnp.float32)

    def early(s):
        scale = active_ref[s * ZH + zh].astype(jnp.float32)
        column = lax.broadcasted_iota(jnp.int32, xs_ref.shape[1:], 1)
        last_quarter = jnp.full(xs_ref.shape[1:], x, jnp.int32) == XS - 1
        past = jnp.logical_and(last_quarter, column >= quarter)
        signal = jnp.where(past, 0.0, xs_ref[s].astype(jnp.float32) * scale)
        for c in range(CH):
            for r in range(nrows):
                rows_ref[s, c, r : r + 1, :] = signal[c : c + 1, r * LANES : (r + 1) * LANES]
        waves = [tg_ref[s, c].astype(jnp.float32) for c in range(CH)]
        for t in range(TPL):
            wave = jnp.concatenate([w[t : t + 1] for w in waves], axis=0)
            wide = jnp.concatenate([wave, jnp.zeros((CH, NF - L), jnp.float32)], axis=1)
            moved_ref[t, 0:CH, :] = pltpu.roll(wide, shift_ref[s * ZH + zh, t], 1)
        for c in range(CH):
            for at in range(0, TPL, 2):
                pair = []
                for slot in (at, at + 1):
                    t = (slot % 16) * 2 + slot // 16
                    wide = jnp.broadcast_to(moved_ref[t, c : c + 1, :], (SUB, NF))
                    pair.append(pltpu.roll(wide, 0, 1, stride=1, stride_axis=0))
                w_ref[s, c, at * SUB : (at + 2) * SUB, :] = jnp.concatenate(
                    pair, axis=0).astype(jnp.bfloat16)
            multiply(s, c, 0)

    def late(s):
        for c in range(CH):
            multiply(s, c, 1)

    away = pl.ds(pl.multiple_of((1 - core) * half, SUB), half)
    mine = pl.ds(pl.multiple_of(core * half, SUB), half)

    def to_core(part):
        return pltpu.make_async_remote_copy(
            src_ref=core_send.at[part], dst_ref=core_recv.at[part], send_sem=s1.at[part],
            recv_sem=r1.at[part], device_id=other, device_id_type=MESH)

    def to_y(part, d, py):
        return pltpu.make_async_remote_copy(
            src_ref=y_send.at[part, pl.ds(pl.multiple_of(py * block, block), block)],
            dst_ref=y_recv.at[part, d], send_sem=s2.at[part, d], recv_sem=r2.at[part, d],
            device_id=place(py, z, core), device_id_type=MESH)

    def after_core(part):
        to_core(part).wait()
        total = acc_ref[part, mine] + core_recv[part].astype(jnp.float32)
        sum_ref[part] = total
        y_send[part] = total.astype(jnp.bfloat16)
        for d, py in ys:
            to_y(part, d, py).start()

    gather = []
    for c in range(CH):
        for d in (2, 3, 1):
            gather.append(send(c, wave_ref.at[c], tg_ref.at[x, c], d, XS - d))
    for d in (3, 1, 2):
        for k, (source, target) in enumerate(pieces((x + d) % XS)):
            gather.append(send(CH + k, source, target, d, XS - d))
    pl.semaphore_wait(barrier, len(targets))
    for copy in gather:
        copy.start()
    tell(1)
    for copy in local:
        copy.wait()

    def arrive(step, carry):
        offset = step ^ (step // 2)
        s = (x + offset) % XS

        @pl.when(step > 0)
        def _():
            for c in range(CH):
                send(c, wave_ref.at[c], tg_ref.at[s, c], 1, offset).wait_recv()

            for k, (source, _) in enumerate(pieces(x)):
                target = xs_ref.at[s, :, k * quarter : k * quarter + source.shape[1]]
                send(CH + k, source, target, 1, offset).wait_recv()

        @pl.when(step == 1)
        def _():
            heard(1)
            tell(2)

        @pl.when(step == 2)
        def _():
            heard(2)
            tell(4)

        early(s)

        @pl.when(step < XS - 1)
        def _():
            late(s)

        return carry

    lax.fori_loop(0, XS, arrive, 0)
    core_send[0] = acc_ref[0, away].astype(jnp.bfloat16)
    to_core(0).start()
    late((x + 2) % XS)
    core_send[1] = acc_ref[1, away].astype(jnp.bfloat16)
    to_core(1).start()
    after_core(0)
    after_core(1)
    for copy in gather:
        copy.wait_send()

    last = [
        pltpu.make_async_remote_copy(
            src_ref=z_send.at[pz], dst_ref=z_recv.at[d], send_sem=s3.at[d], recv_sem=r3.at[d],
            device_id=place(y, pz, core), device_id_type=MESH)
        for d, pz in zs]
    heard(4)
    for part in range(2):
        total = sum_ref[part, pl.ds(pl.multiple_of(y * block, block), block)]
        for d, py in ys:
            to_y(part, d, py).wait()
            total = total + y_recv[part, d].astype(jnp.float32)
        for pzl in range(ZL):
            for k in range(2):
                tile = total[pzl * SUB : (pzl + 1) * SUB, k * LANES : (k + 1) * LANES]
                at = (2 * part + k) * ZL + pzl
                plane_ref[at] = tile
                z_send[at] = tile.astype(jnp.bfloat16)
        for copy, (_, pz) in zip(last, zs):
            pl.when(pz // (nz // 2) == part)(copy.start)

    for copy in last:
        copy.wait()
    total = plane_ref[z]
    for d in range(nz - 1):
        total = total + z_recv[d].astype(jnp.float32)
    out_ref[...] = transpose_groups(total)


def per_device(seismic, templates, moveout, active):
    window = seismic.shape[2]
    span = window // XS + NF
    dma = pltpu.SemaphoreType.DMA
    rows, columns = TPL * SUB, window // XS // SUB // 2
    half = rows // CORES
    block = half // YS
    devices = ZL * ZH
    bf16, f32 = jnp.bfloat16, jnp.float32
    tile = pl.pallas_call(
        stack_kernel,
        out_shape=jax.ShapeDtypeStruct((SUB, LANES), f32),
        in_specs=[pl.BlockSpec(memory_space=pl.ANY)] * 4,
        out_specs=pl.BlockSpec(memory_space=pltpu.VMEM),
        scratch_shapes=[pltpu.SMEM(moveout.shape, moveout.dtype),
                        pltpu.SMEM(active.shape, active.dtype),
                        pltpu.VMEM((XS, CH, span), bf16),
                        pltpu.VMEM((XS, CH, TPL, L), bf16),
                        dma((CH + 2, XS)), dma((CH + 2, XS)), dma((5,)),
                        pltpu.VMEM((XS, CH, 40, LANES), f32),
                        pltpu.VMEM((TPL, SUB, NF), f32),
                        pltpu.VMEM((XS, CH, rows, NF), bf16),
                        pltpu.VMEM((columns, NF), bf16),
                        pltpu.VMEM((2, rows, columns), f32),
                        pltpu.VMEM((2, half, columns), bf16),
                        pltpu.VMEM((2, half, columns), bf16),
                        pltpu.VMEM((2, half, columns), f32),
                        pltpu.VMEM((2, half, columns), bf16),
                        pltpu.VMEM((2, YS - 1, block, columns), bf16),
                        pltpu.VMEM((devices, SUB, LANES), f32),
                        pltpu.VMEM((devices, SUB, LANES), bf16),
                        pltpu.VMEM((devices - 1, SUB, LANES), bf16),
                        dma((2,)), dma((2,)), dma((2, YS - 1)), dma((2, YS - 1)),
                        dma((devices - 1,)), dma((devices - 1,)),
                        pltpu.SemaphoreType.REGULAR((3,))],
        compiler_params=pltpu.CompilerParams(collective_id=0, has_side_effects=True),
        name="stack",
    )(moveout, active, seismic[0], templates[0].transpose(1, 0, 2))
    return tile.reshape(1, SUB * LANES)


def solution(mesh):
    in_specs = (
        P(("tmpl", "tm"), None, None),
        P(("tmpl", "tm"), None, None, None),
        P("tmpl", None),
        P("tmpl"),
    )
    out_specs = P("tmpl", "tm")
    return jax.shard_map(
        per_device, mesh=mesh, in_specs=in_specs, out_specs=out_specs, check_vma=False
    )
```
